128 devices in a mesh: pencil: 16 (over z, y_lo, core), group: 8 (over y_hi, x).
Axes of the slice: x: 4, y: 4 (y_hi: 2, y_lo: 2; y = y_hi * 2 + y_lo), z: 4, core: 2. Of those that a mesh axis runs over, the one named last changes fastest.
Arguments:
- velocity: float32 [49152, 3, 512], P(('pencil', 'group')), may hold values from -6 to 6
- viscosity: float32 [49152, 512], P(('pencil', 'group')), may hold values from 300 to 10000
- density: float32 [49152, 512], P(('pencil', 'group')), may hold values from 0.5 to 2
- slot_block: int32 [49152], P(('pencil', 'group')), may hold values from -1 to 49151, as said below
Outputs:
- velocity_out: float32 [3, 384, 65536], P(None, 'pencil', 'group')
The draws below stay inside these ranges and needn't reach their ends.
Inputs may be any that keep to these rules, and one draw needn't show every extreme that they name: `slot_block`: -1 marks an empty slot; otherwise the entry is a block number l * 48 + j. Each block appears in at most one slot, and a block is active exactly if it appears. The line layout gives block (l, j) to device index (j // 3) * 8 + l // 128 of pencil+group; the live slots of one device hold at most 3 blocks of any one device of the line layout. The active blocks of each line of blocks form one run along x that contains x blocks 48 // 4 to 35.
All inputs are finite; a program needn't handle non-finite values.
Results may differ from the reference program's by a relative error of at most 0.0003.
Values sent between devices are 32-bit elements; how exact they have to be, the bound alone decides.
A program may use at most 128 MiB of HBM per device.

```python
import math
import jax
import jax.numpy as jnp
from jax import lax

EDGE = 8
CELLS = 512
BX_SEG = 3
LB_DEV = 128
NBX = 48
NLB = 1024
NX = 384
NL = 65536
SLOT_DEV = 384
SLOTS = 49152
N_GROUP = 8
DEVICES = 128


def alternate(block_x, block_y, block_z):
    morton_code = jnp.zeros_like(block_x)
    for bit_index in range(10):
        morton_code = morton_code | (block_x >> bit_index & 1) << 3 * bit_index
        morton_code = morton_code | (block_y >> bit_index & 1) << 3 * bit_index + 1
        morton_code = morton_code | (block_z >> bit_index & 1) << 3 * bit_index + 2
    return morton_code


def order_rank(group_key, morton_rank, count_all):
    composite = group_key * count_all + morton_rank
    sorted_order = jnp.argsort(composite)
    group_sizes = jnp.zeros((DEVICES + 1,), jnp.int32).at[group_key].add(1)
    starts = jnp.cumsum(group_sizes) - group_sizes
    rank_sorted = jnp.arange(count_all, dtype=jnp.int32) - starts[group_key[sorted_order]]
    return jnp.zeros((count_all,), jnp.int32).at[sorted_order].set(rank_sorted)


def draw_slot_block(key, part):
    key_low, key_high, key_turn = jax.random.split(key, 3)
    count_all = NBX * NLB
    block_ids = jnp.arange(count_all, dtype=jnp.int32)
    block_line = block_ids // NBX
    block_x = block_ids % NBX
    run_start = jax.random.randint(key_low, (NLB,), 0, NBX // 4 + 1)
    run_end = NBX - jax.random.randint(key_high, (NLB,), 0, NBX // 4 + 1)
    active = (block_x >= run_start[block_line]) & (block_x < run_end[block_line])
    target = block_x // BX_SEG * N_GROUP + block_line // LB_DEV
    morton_code = alternate(block_x, block_line % 16, block_line // 16)
    morton_rank = jnp.zeros((count_all,), jnp.int32).at[jnp.argsort(morton_code)].set(block_ids)
    target_key = jnp.where(active, target, DEVICES).astype(jnp.int32)
    within = order_rank(target_key, morton_rank, count_all)
    turn_offset = jax.random.randint(key_turn, (DEVICES + 1,), 0, DEVICES)
    owner_dev = (within + turn_offset[target_key]) % DEVICES
    owner_key = jnp.where(active, owner_dev, DEVICES).astype(jnp.int32)
    slot_index = order_rank(owner_key, morton_rank, count_all)
    place_at = jnp.where(active, owner_dev * SLOT_DEV + slot_index, SLOTS).astype(jnp.int32)
    return jnp.full((SLOTS,), -1, jnp.int32).at[place_at].set(block_ids, mode='drop')


def draw_velocity(key, part):
    values = jax.random.normal(key, (SLOTS, 3, CELLS), jnp.float32)
    return jnp.clip(values, -6.0, 6.0)


def draw_viscosity(key, part):
    low_end = 300.0
    high_end = 3000.0
    return jnp.exp(jax.random.uniform(key, (SLOTS, CELLS), jnp.float32, math.log(low_end), math.log(high_end)))


def steps_of(own_key, shape, cuts, least, largest):
    gain = 1.0
    for axis_at, blocks in cuts:
        steps = jax.random.uniform(jax.random.fold_in(jax.random.fold_in(own_key, 6), axis_at), (blocks,), jnp.float32, least / len(cuts), largest / len(cuts))
        gain = gain * jnp.repeat(jnp.exp(steps), shape[axis_at] // blocks).reshape((-1,) + (1,) * (len(shape) - 1 - axis_at))
    return gain


def setup_inputs(seed: int = 0) -> dict:
    key_of = jax.random.split(jax.random.key(seed), 5)
    return {
        "velocity": draw_velocity(jax.random.fold_in(key_of[4], 71), 0),
        "viscosity": draw_viscosity(jax.random.fold_in(key_of[4], 71), 0),
        "density": jnp.clip(jnp.exp(math.log(2.0) - 1.3862944 * jax.random.uniform(key_of[2], (SLOTS, CELLS), jnp.float32) ** steps_of(key_of[2], (SLOTS, CELLS), ((0, 128),), -0.2, 0.2)), 0.5, 2.0),
        "slot_block": draw_slot_block(jax.random.fold_in(key_of[4], 71), 0),
    }


def spread_fields(velocity, viscosity, density, slot_block):
    count_blocks = NBX * NLB
    live_slot = slot_block >= 0
    target = jnp.where(live_slot, slot_block, count_blocks).astype(jnp.int32)
    fields = jnp.concatenate([velocity, viscosity[:, None, :], density[:, None, :]], axis=1)
    dense_fields = jnp.zeros((count_blocks, 5, CELLS), jnp.float32).at[target].set(fields, mode='drop')
    block_active = jnp.zeros((count_blocks,), jnp.float32).at[target].set(1.0, mode='drop')
    grid_fields = dense_fields.reshape(NLB, NBX, 5, EDGE, EDGE * EDGE).transpose(1, 3, 2, 0, 4).reshape(NX, 5, NL)
    active = jnp.broadcast_to(block_active.reshape(NLB, NBX).T[:, None, :, None], (NBX, EDGE, NLB, EDGE * EDGE)).reshape(NX, NL)
    return (grid_fields, active)

def reference(velocity, viscosity, density, slot_block):
    grid_fields, active = spread_fields(velocity, viscosity, density, slot_block)
    velocity_grid = grid_fields[:, 0:3, :]
    visc_grid = grid_fields[:, 3, :]
    mass_grid = grid_fields[:, 4, :]
    inner_faces = 0.5 * (visc_grid[:-1] + visc_grid[1:]) * active[:-1] * active[1:]
    edge_zero = jnp.zeros((1, NL), jnp.float32)
    face_left = jnp.concatenate([edge_zero, inner_faces], axis=0)
    face_right = jnp.concatenate([inner_faces, edge_zero], axis=0)
    main_band = mass_grid + face_left + face_right + (1.0 - active)
    right_side = mass_grid[:, None, :] * velocity_grid
    solved = lax.linalg.tridiagonal_solve((-face_left).T, main_band.T, (-face_right).T, right_side.transpose(2, 0, 1))
    return solved.transpose(2, 1, 0)
```

```python
import jax
import jax.numpy as jnp
from jax import lax
from jax.sharding import PartitionSpec as P

EDGE = 8
CELLS = 512
BX_SEG = 3
LB_DEV = 128
BPD = 384


def shifted(value, axis, steps):
    count = lax.axis_size(axis)
    first, last = (max(0, -steps), min(count, count - steps))
    return lax.ppermute(value, axis, [(source, source + steps) for source in range(first, last)])


def padded(block, sides, width):
    for axis, dim in sides:
        count = lax.axis_size(axis)
        forward = [(i, i + 1) for i in range(count - 1)]
        backward = [(target, source) for source, target in forward]
        low = lax.ppermute(
            lax.slice_in_dim(block, block.shape[dim] - width, None, axis=dim), axis, forward
        )
        high = lax.ppermute(lax.slice_in_dim(block, 0, width, axis=dim), axis, backward)
        block = jnp.concatenate([low, block, high], axis=dim)
    return block


def combine_rows(row_set, before, after_rows, left_ok, right_ok):
    alpha = jnp.where(
        left_ok, -row_set[..., 0, :] / jnp.where(left_ok, before[..., 1, :], 1.0), 0.0
    )
    gamma = jnp.where(
        right_ok, -row_set[..., 2, :] / jnp.where(right_ok, after_rows[..., 1, :], 1.0), 0.0
    )
    new_lower = alpha * before[..., 0, :]
    new_upper = gamma * after_rows[..., 2, :]
    new_main = row_set[..., 1, :] + alpha * before[..., 2, :] + gamma * after_rows[..., 0, :]
    new_right = (
        row_set[..., 3:, :]
        + alpha[..., None, :] * before[..., 3:, :]
        + gamma[..., None, :] * after_rows[..., 3:, :]
    )
    return jnp.concatenate(
        [new_lower[..., None, :], new_main[..., None, :], new_upper[..., None, :], new_right],
        axis=-2,
    )


def neighbours(left_part, right_part, offset):
    from_left = shifted(left_part, "pencil", offset)
    from_right = shifted(right_part, "pencil", -offset)
    return (from_left, from_right)


def on_device(velocity, viscosity, density, slot_block):
    n_pencil = lax.axis_size("pencil")
    n_group = lax.axis_size("group")
    devices = n_pencil * n_group
    n_slots = slot_block.shape[0]
    capacity = n_slots // devices
    blocks_x = BX_SEG * n_pencil
    edge_sq = EDGE * EDGE
    seg_width = EDGE * BX_SEG
    lines_here = LB_DEV * edge_sq
    live_slot = slot_block >= 0
    safe_ids = jnp.where(live_slot, slot_block, 0)
    block_x = safe_ids % blocks_x
    block_line = safe_ids // blocks_x
    target = block_x // BX_SEG * n_group + block_line // LB_DEV
    one_hot = jnp.logical_and(
        target[:, None] == jnp.arange(devices, dtype=jnp.int32)[None, :], live_slot[:, None]
    ).astype(jnp.int32)
    target_rank = jnp.sum((jnp.cumsum(one_hot, axis=0) - 1) * one_hot, axis=1)
    position = jnp.where(live_slot, target * capacity + target_rank, devices * capacity)
    source_of = (
        jnp.full((devices * capacity,), n_slots, jnp.int32)
        .at[position]
        .set(jnp.arange(n_slots, dtype=jnp.int32), mode="drop")
    )
    send_flow = jnp.take(velocity, source_of, axis=0, mode="fill", fill_value=0.0)
    send_visc = jnp.take(viscosity, source_of, axis=0, mode="fill", fill_value=0.0)
    send_mass = jnp.take(density, source_of, axis=0, mode="fill", fill_value=0.0)
    labels = jnp.take(slot_block, source_of, axis=0, mode="fill", fill_value=-1)
    got_flow, got_visc, got_mass, arrived_ids = (
        lax.all_to_all(
            send_flow.reshape(devices, capacity, 3, CELLS),
            ("pencil", "group"),
            split_axis=0,
            concat_axis=0,
            tiled=True,
        ),
        lax.all_to_all(
            send_visc.reshape(devices, capacity, CELLS),
            ("pencil", "group"),
            split_axis=0,
            concat_axis=0,
            tiled=True,
        ),
        lax.all_to_all(
            send_mass.reshape(devices, capacity, CELLS),
            ("pencil", "group"),
            split_axis=0,
            concat_axis=0,
            tiled=True,
        ),
        lax.all_to_all(
            labels.reshape(devices, capacity),
            ("pencil", "group"),
            split_axis=0,
            concat_axis=0,
            tiled=True,
        ),
    )
    n_arrived = devices * capacity
    got_flow = got_flow.reshape(n_arrived, 3, CELLS)
    got_visc = got_visc.reshape(n_arrived, CELLS)
    got_mass = got_mass.reshape(n_arrived, CELLS)
    arrived_ids = arrived_ids.reshape(n_arrived)
    pencil_at = lax.axis_index("pencil")
    group_at = lax.axis_index("group")
    arrive_live = arrived_ids >= 0
    arrive_safe = jnp.where(arrive_live, arrived_ids, 0)
    local_block = (arrive_safe // blocks_x - group_at * LB_DEV) * BX_SEG + (
        arrive_safe % blocks_x - pencil_at * BX_SEG
    )
    local_block = jnp.where(arrive_live, local_block, BPD).astype(jnp.int32)
    which_arrived = (
        jnp.full((BPD,), n_arrived, jnp.int32)
        .at[local_block]
        .set(jnp.arange(n_arrived, dtype=jnp.int32), mode="drop")
    )
    block_active = (which_arrived < n_arrived).astype(jnp.float32)
    tile_flow = jnp.take(got_flow, which_arrived, axis=0, mode="fill", fill_value=0.0)
    tile_visc = jnp.take(got_visc, which_arrived, axis=0, mode="fill", fill_value=0.0)
    tile_mass = jnp.take(got_mass, which_arrived, axis=0, mode="fill", fill_value=0.0)
    flow_grid = (
        tile_flow.reshape(LB_DEV, BX_SEG, 3, EDGE, edge_sq)
        .transpose(2, 1, 3, 0, 4)
        .reshape(3, seg_width, lines_here)
    )
    visc_grid = (
        tile_visc.reshape(LB_DEV, BX_SEG, EDGE, edge_sq)
        .transpose(1, 2, 0, 3)
        .reshape(seg_width, lines_here)
    )
    mass_grid = (
        tile_mass.reshape(LB_DEV, BX_SEG, EDGE, edge_sq)
        .transpose(1, 2, 0, 3)
        .reshape(seg_width, lines_here)
    )
    active = jnp.broadcast_to(
        block_active.reshape(LB_DEV, BX_SEG).T[:, None, :, None], (BX_SEG, EDGE, LB_DEV, edge_sq)
    ).reshape(seg_width, lines_here)
    rimmed = padded(jnp.stack([visc_grid, active], axis=0), (("pencil", 1),), 1)
    face_visc = 0.5 * (rimmed[0, :-1] + rimmed[0, 1:]) * rimmed[1, :-1] * rimmed[1, 1:]
    face_left = face_visc[:-1]
    face_right = face_visc[1:]
    lower_band = -face_left
    upper_band = -face_right
    main_band = mass_grid + face_left + face_right + (1.0 - active)
    right_side = mass_grid[None] * flow_grid
    prev_lower = -jnp.ones((lines_here,), jnp.float32)
    prev_upper = jnp.zeros((lines_here,), jnp.float32)
    prev_right = jnp.zeros((3, lines_here), jnp.float32)
    fwd_lower, fwd_upper, fwd_right = ([], [], [])
    for cell_x in range(1, seg_width):
        low_coef = lower_band[cell_x]
        pivot_inv = 1.0 / (main_band[cell_x] - low_coef * prev_upper)
        prev_lower = -low_coef * prev_lower * pivot_inv
        prev_upper = upper_band[cell_x] * pivot_inv
        prev_right = (right_side[:, cell_x] - low_coef[None, :] * prev_right) * pivot_inv[None, :]
        fwd_lower.append(prev_lower)
        fwd_upper.append(prev_upper)
        fwd_right.append(prev_right)
    next_lower = jnp.zeros((lines_here,), jnp.float32)
    next_upper = -jnp.ones((lines_here,), jnp.float32)
    next_right = jnp.zeros((3, lines_here), jnp.float32)
    back_lower = [None] * (seg_width - 2)
    back_upper = [None] * (seg_width - 2)
    back_right = [None] * (seg_width - 2)
    for index_k in range(seg_width - 3, -1, -1):
        row_upper = fwd_upper[index_k]
        next_right = fwd_right[index_k] - row_upper[None, :] * next_right
        next_lower = fwd_lower[index_k] - row_upper * next_lower
        next_upper = -row_upper * next_upper
        back_lower[index_k] = next_lower
        back_upper[index_k] = next_upper
        back_right[index_k] = next_right
    first_row = jnp.concatenate(
        [
            lower_band[0][None],
            (main_band[0] - upper_band[0] * back_lower[0])[None],
            (-upper_band[0] * back_upper[0])[None],
            right_side[:, 0] - upper_band[0][None, :] * back_right[0],
        ],
        axis=0,
    )
    last_row = jnp.concatenate(
        [
            fwd_lower[-1][None],
            jnp.ones((1, lines_here), jnp.float32),
            fwd_upper[-1][None],
            fwd_right[-1],
        ],
        axis=0,
    )
    reduced = jnp.stack([first_row, last_row])
    chunk = lines_here // n_pencil
    sent_rows = reduced.reshape(2, 6, n_pencil, chunk).transpose(2, 0, 1, 3)
    all_rows = lax.all_to_all(sent_rows, "pencil", 0, 0, tiled=True)
    all_rows = all_rows.reshape(2 * n_pencil, 6, chunk)
    scaled_upper = []
    scaled_right = []
    carry_upper = jnp.zeros((chunk,), jnp.float32)
    carry_right = jnp.zeros((3, chunk), jnp.float32)
    for row_at in range(2 * n_pencil):
        row_lower = all_rows[row_at, 0]
        row_inv = 1.0 / (all_rows[row_at, 1] - row_lower * carry_upper)
        carry_upper = all_rows[row_at, 2] * row_inv
        carry_right = (all_rows[row_at, 3:] - row_lower[None, :] * carry_right) * row_inv[None, :]
        scaled_upper.append(carry_upper)
        scaled_right.append(carry_right)
    ends = [None] * (2 * n_pencil)
    ends[-1] = scaled_right[-1]
    for row_at in range(2 * n_pencil - 2, -1, -1):
        ends[row_at] = scaled_right[row_at] - scaled_upper[row_at][None, :] * ends[row_at + 1]
    solved_ends = jnp.stack(ends).reshape(n_pencil, 2, 3, chunk)
    solved_ends = lax.all_to_all(solved_ends, "pencil", 0, 0, tiled=True)
    solution_ends = solved_ends.transpose(1, 2, 0, 3).reshape(2, 3, lines_here)
    end_first = solution_ends[0]
    end_last = solution_ends[1]
    columns = [end_first]
    for index_k in range(seg_width - 2):
        columns.append(
            back_right[index_k]
            - back_lower[index_k][None, :] * end_first
            - back_upper[index_k][None, :] * end_last
        )
    columns.append(end_last)
    return jnp.stack(columns, axis=1)


def solution(mesh):
    in_specs = (
        P(("pencil", "group"), None, None),
        P(("pencil", "group"), None),
        P(("pencil", "group"), None),
        P(("pencil", "group")),
    )
    out_specs = P(None, "pencil", "group")
    return jax.shard_map(
        on_device, mesh=mesh, in_specs=in_specs, out_specs=out_specs, check_vma=False
    )
```

```python
import jax
import jax.numpy as jnp
from jax import lax
from jax.sharding import PartitionSpec as P

EDGE = 8
CELLS = 512
BX_SEG = 3
LB_DEV = 128
BPD = 384


def shifted(value, axis, steps):
    count = lax.axis_size(axis)
    first, last = (max(0, -steps), min(count, count - steps))
    return lax.ppermute(value, axis, [(source, source + steps) for source in range(first, last)])


def padded(block, sides, width):
    for axis, dim in sides:
        count = lax.axis_size(axis)
        forward = [(i, i + 1) for i in range(count - 1)]
        backward = [(target, source) for source, target in forward]
        low = lax.ppermute(
            lax.slice_in_dim(block, block.shape[dim] - width, None, axis=dim), axis, forward
        )
        high = lax.ppermute(lax.slice_in_dim(block, 0, width, axis=dim), axis, backward)
        block = jnp.concatenate([low, block, high], axis=dim)
    return block


def combine_rows(row_set, before, after_rows, left_ok, right_ok):
    alpha = jnp.where(
        left_ok, -row_set[..., 0, :] / jnp.where(left_ok, before[..., 1, :], 1.0), 0.0
    )
    gamma = jnp.where(
        right_ok, -row_set[..., 2, :] / jnp.where(right_ok, after_rows[..., 1, :], 1.0), 0.0
    )
    new_lower = alpha * before[..., 0, :]
    new_upper = gamma * after_rows[..., 2, :]
    new_main = row_set[..., 1, :] + alpha * before[..., 2, :] + gamma * after_rows[..., 0, :]
    new_right = (
        row_set[..., 3:, :]
        + alpha[..., None, :] * before[..., 3:, :]
        + gamma[..., None, :] * after_rows[..., 3:, :]
    )
    return jnp.concatenate(
        [new_lower[..., None, :], new_main[..., None, :], new_upper[..., None, :], new_right],
        axis=-2,
    )


def neighbours(left_part, right_part, offset):
    from_left = shifted(left_part, "pencil", offset)
    from_right = shifted(right_part, "pencil", -offset)
    return (from_left, from_right)


def on_device(velocity, viscosity, density, slot_block):
    n_pencil = lax.axis_size("pencil")
    n_group = lax.axis_size("group")
    devices = n_pencil * n_group
    n_slots = slot_block.shape[0]
    capacity = n_slots // devices
    blocks_x = BX_SEG * n_pencil
    edge_sq = EDGE * EDGE
    seg_width = EDGE * BX_SEG
    lines_here = LB_DEV * edge_sq
    live_slot = slot_block >= 0
    safe_ids = jnp.where(live_slot, slot_block, 0)
    block_x = safe_ids % blocks_x
    block_line = safe_ids // blocks_x
    target = block_x // BX_SEG * n_group + block_line // LB_DEV
    one_hot = jnp.logical_and(
        target[:, None] == jnp.arange(devices, dtype=jnp.int32)[None, :], live_slot[:, None]
    ).astype(jnp.int32)
    target_rank = jnp.sum((jnp.cumsum(one_hot, axis=0) - 1) * one_hot, axis=1)
    position = jnp.where(live_slot, target * capacity + target_rank, devices * capacity)
    source_of = (
        jnp.full((devices * capacity,), n_slots, jnp.int32)
        .at[position]
        .set(jnp.arange(n_slots, dtype=jnp.int32), mode="drop")
    )
    width = 5 * CELLS
    fields = jnp.concatenate(
        [
            velocity.reshape(n_slots, 3 * CELLS),
            viscosity,
            density,
            jnp.broadcast_to(slot_block.astype(jnp.float32)[:, None], (n_slots, 128)),
        ],
        axis=1,
    )
    send_all = jnp.take(fields, source_of, axis=0, mode="fill", fill_value=-1.0)
    got_all = lax.all_to_all(
        send_all.reshape(devices, capacity, width + 128),
        ("pencil", "group"),
        split_axis=0,
        concat_axis=0,
        tiled=True,
    )
    n_arrived = devices * capacity
    got_all = got_all.reshape(n_arrived, width + 128)
    arrived_ids = got_all[:, width].astype(jnp.int32)
    pencil_at = lax.axis_index("pencil")
    group_at = lax.axis_index("group")
    arrive_live = arrived_ids >= 0
    arrive_safe = jnp.where(arrive_live, arrived_ids, 0)
    local_block = (arrive_safe // blocks_x - group_at * LB_DEV) * BX_SEG + (
        arrive_safe % blocks_x - pencil_at * BX_SEG
    )
    local_block = jnp.where(arrive_live, local_block, BPD).astype(jnp.int32)
    which_arrived = (
        jnp.full((BPD,), n_arrived, jnp.int32)
        .at[local_block]
        .set(jnp.arange(n_arrived, dtype=jnp.int32), mode="drop")
    )
    block_active = (which_arrived < n_arrived).astype(jnp.float32)
    tiles = jnp.take(got_all[:, :width], which_arrived, axis=0, mode="fill", fill_value=0.0)
    grid = (
        tiles.reshape(LB_DEV, BX_SEG, 5, EDGE, edge_sq)
        .transpose(2, 1, 3, 0, 4)
        .reshape(5, seg_width, lines_here)
    )
    flow_grid = grid[:3]
    visc_grid = grid[3]
    mass_grid = grid[4]
    active = jnp.broadcast_to(
        block_active.reshape(LB_DEV, BX_SEG).T[:, None, :, None], (BX_SEG, EDGE, LB_DEV, edge_sq)
    ).reshape(seg_width, lines_here)
    rimmed = padded(jnp.stack([visc_grid, active], axis=0), (("pencil", 1),), 1)
    face_visc = 0.5 * (rimmed[0, :-1] + rimmed[0, 1:]) * rimmed[1, :-1] * rimmed[1, 1:]
    face_left = face_visc[:-1]
    face_right = face_visc[1:]
    lower_band = -face_left
    upper_band = -face_right
    main_band = mass_grid + face_left + face_right + (1.0 - active)
    right_side = mass_grid[None] * flow_grid
    prev_lower = -jnp.ones((lines_here,), jnp.float32)
    prev_upper = jnp.zeros((lines_here,), jnp.float32)
    prev_right = jnp.zeros((3, lines_here), jnp.float32)
    fwd_lower, fwd_upper, fwd_right = ([], [], [])
    for cell_x in range(1, seg_width):
        low_coef = lower_band[cell_x]
        pivot_inv = 1.0 / (main_band[cell_x] - low_coef * prev_upper)
        prev_lower = -low_coef * prev_lower * pivot_inv
        prev_upper = upper_band[cell_x] * pivot_inv
        prev_right = (right_side[:, cell_x] - low_coef[None, :] * prev_right) * pivot_inv[None, :]
        fwd_lower.append(prev_lower)
        fwd_upper.append(prev_upper)
        fwd_right.append(prev_right)
    next_lower = jnp.zeros((lines_here,), jnp.float32)
    next_upper = -jnp.ones((lines_here,), jnp.float32)
    next_right = jnp.zeros((3, lines_here), jnp.float32)
    back_lower = [None] * (seg_width - 2)
    back_upper = [None] * (seg_width - 2)
    back_right = [None] * (seg_width - 2)
    for index_k in range(seg_width - 3, -1, -1):
        row_upper = fwd_upper[index_k]
        next_right = fwd_right[index_k] - row_upper[None, :] * next_right
        next_lower = fwd_lower[index_k] - row_upper * next_lower
        next_upper = -row_upper * next_upper
        back_lower[index_k] = next_lower
        back_upper[index_k] = next_upper
        back_right[index_k] = next_right
    first_row = jnp.concatenate(
        [
            lower_band[0][None],
            (main_band[0] - upper_band[0] * back_lower[0])[None],
            (-upper_band[0] * back_upper[0])[None],
            right_side[:, 0] - upper_band[0][None, :] * back_right[0],
        ],
        axis=0,
    )
    last_row = jnp.concatenate(
        [
            fwd_lower[-1][None],
            jnp.ones((1, lines_here), jnp.float32),
            fwd_upper[-1][None],
            fwd_right[-1],
        ],
        axis=0,
    )
    reduced = jnp.stack([first_row, last_row])
    chunk = lines_here // n_pencil
    sent_rows = reduced.reshape(2, 6, n_pencil, chunk).transpose(2, 0, 1, 3)
    all_rows = lax.all_to_all(sent_rows, "pencil", 0, 0, tiled=True)
    all_rows = all_rows.reshape(2 * n_pencil, 6, chunk)
    scaled_upper = []
    scaled_right = []
    carry_upper = jnp.zeros((chunk,), jnp.float32)
    carry_right = jnp.zeros((3, chunk), jnp.float32)
    for row_at in range(2 * n_pencil):
        row_lower = all_rows[row_at, 0]
        row_inv = 1.0 / (all_rows[row_at, 1] - row_lower * carry_upper)
        carry_upper = all_rows[row_at, 2] * row_inv
        carry_right = (all_rows[row_at, 3:] - row_lower[None, :] * carry_right) * row_inv[None, :]
        scaled_upper.append(carry_upper)
        scaled_right.append(carry_right)
    ends = [None] * (2 * n_pencil)
    ends[-1] = scaled_right[-1]
    for row_at in range(2 * n_pencil - 2, -1, -1):
        ends[row_at] = scaled_right[row_at] - scaled_upper[row_at][None, :] * ends[row_at + 1]
    solved_ends = jnp.stack(ends).reshape(n_pencil, 2, 3, chunk)
    solved_ends = lax.all_to_all(solved_ends, "pencil", 0, 0, tiled=True)
    solution_ends = solved_ends.transpose(1, 2, 0, 3).reshape(2, 3, lines_here)
    end_first = solution_ends[0]
    end_last = solution_ends[1]
    columns = [end_first]
    for index_k in range(seg_width - 2):
        columns.append(
            back_right[index_k]
            - back_lower[index_k][None, :] * end_first
            - back_upper[index_k][None, :] * end_last
        )
    columns.append(end_last)
    return jnp.stack(columns, axis=1)


def solution(mesh):
    in_specs = (
        P(("pencil", "group"), None, None),
        P(("pencil", "group"), None),
        P(("pencil", "group"), None),
        P(("pencil", "group")),
    )
    out_specs = P(None, "pencil", "group")
    return jax.shard_map(
        on_device, mesh=mesh, in_specs=in_specs, out_specs=out_specs, check_vma=False
    )
```

```python
import jax
import jax.numpy as jnp
from jax import lax
from jax.sharding import PartitionSpec as P

EDGE = 8
CELLS = 512
BX_SEG = 3
LB_DEV = 128
BPD = 384


def shifted(value, axis, steps):
    count = lax.axis_size(axis)
    first, last = (max(0, -steps), min(count, count - steps))
    return lax.ppermute(value, axis, [(source, source + steps) for source in range(first, last)])


def padded(block, sides, width):
    for axis, dim in sides:
        count = lax.axis_size(axis)
        forward = [(i, i + 1) for i in range(count - 1)]
        backward = [(target, source) for source, target in forward]
        low = lax.ppermute(
            lax.slice_in_dim(block, block.shape[dim] - width, None, axis=dim), axis, forward
        )
        high = lax.ppermute(lax.slice_in_dim(block, 0, width, axis=dim), axis, backward)
        block = jnp.concatenate([low, block, high], axis=dim)
    return block


def combine_rows(row_set, before, after_rows, left_ok, right_ok):
    alpha = jnp.where(
        left_ok, -row_set[..., 0, :] / jnp.where(left_ok, before[..., 1, :], 1.0), 0.0
    )
    gamma = jnp.where(
        right_ok, -row_set[..., 2, :] / jnp.where(right_ok, after_rows[..., 1, :], 1.0), 0.0
    )
    new_lower = alpha * before[..., 0, :]
    new_upper = gamma * after_rows[..., 2, :]
    new_main = row_set[..., 1, :] + alpha * before[..., 2, :] + gamma * after_rows[..., 0, :]
    new_right = (
        row_set[..., 3:, :]
        + alpha[..., None, :] * before[..., 3:, :]
        + gamma[..., None, :] * after_rows[..., 3:, :]
    )
    return jnp.concatenate(
        [new_lower[..., None, :], new_main[..., None, :], new_upper[..., None, :], new_right],
        axis=-2,
    )


def neighbours(left_part, right_part, offset):
    from_left = shifted(left_part, "pencil", offset)
    from_right = shifted(right_part, "pencil", -offset)
    return (from_left, from_right)


def on_device(velocity, viscosity, density, slot_block):
    n_pencil = lax.axis_size("pencil")
    n_group = lax.axis_size("group")
    devices = n_pencil * n_group
    n_slots = slot_block.shape[0]
    capacity = n_slots // devices
    blocks_x = BX_SEG * n_pencil
    edge_sq = EDGE * EDGE
    seg_width = EDGE * BX_SEG
    lines_here = LB_DEV * edge_sq
    live_slot = slot_block >= 0
    safe_ids = jnp.where(live_slot, slot_block, 0)
    block_x = safe_ids % blocks_x
    block_line = safe_ids // blocks_x
    target = block_x // BX_SEG * n_group + block_line // LB_DEV
    one_hot = jnp.logical_and(
        target[:, None] == jnp.arange(devices, dtype=jnp.int32)[None, :], live_slot[:, None]
    ).astype(jnp.int32)
    target_rank = jnp.sum((jnp.cumsum(one_hot, axis=0) - 1) * one_hot, axis=1)
    position = jnp.where(live_slot, target * capacity + target_rank, devices * capacity)
    source_of = (
        jnp.full((devices * capacity,), n_slots, jnp.int32)
        .at[position]
        .set(jnp.arange(n_slots, dtype=jnp.int32), mode="drop")
    )
    width = 5 * CELLS
    fields = jnp.concatenate(
        [velocity, viscosity[:, None, :], density[:, None, :]], axis=1
    ).reshape(n_slots, width)
    send_all = jnp.take(fields, source_of, axis=0, mode="fill", fill_value=0.0)
    got_all = lax.all_to_all(
        send_all.reshape(devices, capacity, width),
        ("pencil", "group"),
        split_axis=0,
        concat_axis=0,
        tiled=True,
    )
    n_arrived = devices * capacity
    got_all = got_all.reshape(n_arrived, width)
    pencil_at = lax.axis_index("pencil")
    group_at = lax.axis_index("group")
    me = pencil_at * n_group + group_at
    all_ids = lax.all_gather(slot_block, ("pencil", "group"), tiled=True)
    all_live = all_ids >= 0
    all_safe = jnp.where(all_live, all_ids, 0)
    all_target = all_safe % blocks_x // BX_SEG * n_group + all_safe // blocks_x // LB_DEV
    mine = jnp.logical_and(all_live, all_target == me).reshape(devices, n_slots)
    mine_rank = jnp.cumsum(mine.astype(jnp.int32), axis=1) - 1
    arrival = jnp.arange(devices, dtype=jnp.int32)[:, None] * capacity + mine_rank
    local_block = (all_safe // blocks_x - group_at * LB_DEV) * BX_SEG + (
        all_safe % blocks_x - pencil_at * BX_SEG
    )
    local_block = jnp.where(mine.reshape(-1), local_block, BPD).astype(jnp.int32)
    which_arrived = (
        jnp.full((BPD,), n_arrived, jnp.int32)
        .at[local_block]
        .set(arrival.reshape(-1), mode="drop")
    )
    block_active = (which_arrived < n_arrived).astype(jnp.float32)
    tiles = jnp.take(got_all, which_arrived, axis=0, mode="fill", fill_value=0.0)
    grid = (
        tiles.reshape(LB_DEV, BX_SEG, 5, EDGE, edge_sq)
        .transpose(2, 1, 3, 0, 4)
        .reshape(5, seg_width, lines_here)
    )
    flow_grid = grid[:3]
    visc_grid = grid[3]
    mass_grid = grid[4]
    active = jnp.broadcast_to(
        block_active.reshape(LB_DEV, BX_SEG).T[:, None, :, None], (BX_SEG, EDGE, LB_DEV, edge_sq)
    ).reshape(seg_width, lines_here)
    rimmed = padded(jnp.stack([visc_grid, active], axis=0), (("pencil", 1),), 1)
    face_visc = 0.5 * (rimmed[0, :-1] + rimmed[0, 1:]) * rimmed[1, :-1] * rimmed[1, 1:]
    face_left = face_visc[:-1]
    face_right = face_visc[1:]
    lower_band = -face_left
    upper_band = -face_right
    main_band = mass_grid + face_left + face_right + (1.0 - active)
    right_side = mass_grid[None] * flow_grid
    prev_lower = -jnp.ones((lines_here,), jnp.float32)
    prev_upper = jnp.zeros((lines_here,), jnp.float32)
    prev_right = jnp.zeros((3, lines_here), jnp.float32)
    fwd_lower, fwd_upper, fwd_right = ([], [], [])
    for cell_x in range(1, seg_width):
        low_coef = lower_band[cell_x]
        pivot_inv = 1.0 / (main_band[cell_x] - low_coef * prev_upper)
        prev_lower = -low_coef * prev_lower * pivot_inv
        prev_upper = upper_band[cell_x] * pivot_inv
        prev_right = (right_side[:, cell_x] - low_coef[None, :] * prev_right) * pivot_inv[None, :]
        fwd_lower.append(prev_lower)
        fwd_upper.append(prev_upper)
        fwd_right.append(prev_right)
    next_lower = jnp.zeros((lines_here,), jnp.float32)
    next_upper = -jnp.ones((lines_here,), jnp.float32)
    next_right = jnp.zeros((3, lines_here), jnp.float32)
    back_lower = [None] * (seg_width - 2)
    back_upper = [None] * (seg_width - 2)
    back_right = [None] * (seg_width - 2)
    for index_k in range(seg_width - 3, -1, -1):
        row_upper = fwd_upper[index_k]
        next_right = fwd_right[index_k] - row_upper[None, :] * next_right
        next_lower = fwd_lower[index_k] - row_upper * next_lower
        next_upper = -row_upper * next_upper
        back_lower[index_k] = next_lower
        back_upper[index_k] = next_upper
        back_right[index_k] = next_right
    first_row = jnp.concatenate(
        [
            lower_band[0][None],
            (main_band[0] - upper_band[0] * back_lower[0])[None],
            (-upper_band[0] * back_upper[0])[None],
            right_side[:, 0] - upper_band[0][None, :] * back_right[0],
        ],
        axis=0,
    )
    last_row = jnp.concatenate(
        [
            fwd_lower[-1][None],
            jnp.ones((1, lines_here), jnp.float32),
            fwd_upper[-1][None],
            fwd_right[-1],
        ],
        axis=0,
    )
    reduced = jnp.stack([first_row, last_row])
    chunk = lines_here // n_pencil
    sent_rows = reduced.reshape(2, 6, n_pencil, chunk).transpose(2, 0, 1, 3)
    all_rows = lax.all_to_all(sent_rows, "pencil", 0, 0, tiled=True)
    all_rows = all_rows.reshape(2 * n_pencil, 6, chunk)
    scaled_upper = []
    scaled_right = []
    carry_upper = jnp.zeros((chunk,), jnp.float32)
    carry_right = jnp.zeros((3, chunk), jnp.float32)
    for row_at in range(2 * n_pencil):
        row_lower = all_rows[row_at, 0]
        row_inv = 1.0 / (all_rows[row_at, 1] - row_lower * carry_upper)
        carry_upper = all_rows[row_at, 2] * row_inv
        carry_right = (all_rows[row_at, 3:] - row_lower[None, :] * carry_right) * row_inv[None, :]
        scaled_upper.append(carry_upper)
        scaled_right.append(carry_right)
    ends = [None] * (2 * n_pencil)
    ends[-1] = scaled_right[-1]
    for row_at in range(2 * n_pencil - 2, -1, -1):
        ends[row_at] = scaled_right[row_at] - scaled_upper[row_at][None, :] * ends[row_at + 1]
    solved_ends = jnp.stack(ends).reshape(n_pencil, 2, 3, chunk)
    solved_ends = lax.all_to_all(solved_ends, "pencil", 0, 0, tiled=True)
    solution_ends = solved_ends.transpose(1, 2, 0, 3).reshape(2, 3, lines_here)
    end_first = solution_ends[0]
    end_last = solution_ends[1]
    columns = [end_first]
    for index_k in range(seg_width - 2):
        columns.append(
            back_right[index_k]
            - back_lower[index_k][None, :] * end_first
            - back_upper[index_k][None, :] * end_last
        )
    columns.append(end_last)
    return jnp.stack(columns, axis=1)


def solution(mesh):
    in_specs = (
        P(("pencil", "group"), None, None),
        P(("pencil", "group"), None),
        P(("pencil", "group"), None),
        P(("pencil", "group")),
    )
    out_specs = P(None, "pencil", "group")
    return jax.shard_map(
        on_device, mesh=mesh, in_specs=in_specs, out_specs=out_specs, check_vma=False
    )
```

```python
import jax
import jax.numpy as jnp
from jax import lax
from jax.sharding import PartitionSpec as P

EDGE = 8
CELLS = 512
BX_SEG = 3
LB_DEV = 128
BPD = 384


def shifted(value, axis, steps):
    count = lax.axis_size(axis)
    first, last = (max(0, -steps), min(count, count - steps))
    return lax.ppermute(value, axis, [(source, source + steps) for source in range(first, last)])


def padded(block, sides, width):
    for axis, dim in sides:
        count = lax.axis_size(axis)
        forward = [(i, i + 1) for i in range(count - 1)]
        backward = [(target, source) for source, target in forward]
        low = lax.ppermute(
            lax.slice_in_dim(block, block.shape[dim] - width, None, axis=dim), axis, forward
        )
        high = lax.ppermute(lax.slice_in_dim(block, 0, width, axis=dim), axis, backward)
        block = jnp.concatenate([low, block, high], axis=dim)
    return block


def combine_rows(row_set, before, after_rows, left_ok, right_ok):
    alpha = jnp.where(
        left_ok, -row_set[..., 0, :] / jnp.where(left_ok, before[..., 1, :], 1.0), 0.0
    )
    gamma = jnp.where(
        right_ok, -row_set[..., 2, :] / jnp.where(right_ok, after_rows[..., 1, :], 1.0), 0.0
    )
    new_lower = alpha * before[..., 0, :]
    new_upper = gamma * after_rows[..., 2, :]
    new_main = row_set[..., 1, :] + alpha * before[..., 2, :] + gamma * after_rows[..., 0, :]
    new_right = (
        row_set[..., 3:, :]
        + alpha[..., None, :] * before[..., 3:, :]
        + gamma[..., None, :] * after_rows[..., 3:, :]
    )
    return jnp.concatenate(
        [new_lower[..., None, :], new_main[..., None, :], new_upper[..., None, :], new_right],
        axis=-2,
    )


def neighbours(left_part, right_part, offset):
    from_left = shifted(left_part, "pencil", offset)
    from_right = shifted(right_part, "pencil", -offset)
    return (from_left, from_right)


def on_device(velocity, viscosity, density, slot_block):
    n_pencil = lax.axis_size("pencil")
    n_group = lax.axis_size("group")
    devices = n_pencil * n_group
    n_slots = slot_block.shape[0]
    capacity = n_slots // devices
    blocks_x = BX_SEG * n_pencil
    edge_sq = EDGE * EDGE
    seg_width = EDGE * BX_SEG
    lines_here = LB_DEV * edge_sq
    live_slot = slot_block >= 0
    safe_ids = jnp.where(live_slot, slot_block, 0)
    block_x = safe_ids % blocks_x
    block_line = safe_ids // blocks_x
    target = block_x // BX_SEG * n_group + block_line // LB_DEV
    one_hot = jnp.logical_and(
        target[:, None] == jnp.arange(devices, dtype=jnp.int32)[None, :], live_slot[:, None]
    ).astype(jnp.int32)
    target_rank = jnp.sum((jnp.cumsum(one_hot, axis=0) - 1) * one_hot, axis=1)
    position = jnp.where(live_slot, target * capacity + target_rank, devices * capacity)
    source_of = (
        jnp.full((devices * capacity,), n_slots, jnp.int32)
        .at[position]
        .set(jnp.arange(n_slots, dtype=jnp.int32), mode="drop")
    )
    extras = jnp.stack(
        [
            viscosity,
            density,
            jnp.broadcast_to(slot_block.astype(jnp.float32)[:, None], (n_slots, CELLS)),
        ],
        axis=1,
    )
    send_flow = jnp.take(velocity, source_of, axis=0, mode="fill", fill_value=0.0)
    send_extra = jnp.take(extras, source_of, axis=0, mode="fill", fill_value=-1.0)
    got_flow, got_extra = (
        lax.all_to_all(
            send_flow.reshape(devices, capacity, 3, CELLS),
            ("pencil", "group"),
            split_axis=0,
            concat_axis=0,
            tiled=True,
        ),
        lax.all_to_all(
            send_extra.reshape(devices, capacity, 3, CELLS),
            ("pencil", "group"),
            split_axis=0,
            concat_axis=0,
            tiled=True,
        ),
    )
    n_arrived = devices * capacity
    got_flow = got_flow.reshape(n_arrived, 3, CELLS)
    got_extra = got_extra.reshape(n_arrived, 3, CELLS)
    got_visc = got_extra[:, 0]
    got_mass = got_extra[:, 1]
    arrived_ids = got_extra[:, 2, 0].astype(jnp.int32)
    pencil_at = lax.axis_index("pencil")
    group_at = lax.axis_index("group")
    arrive_live = arrived_ids >= 0
    arrive_safe = jnp.where(arrive_live, arrived_ids, 0)
    local_block = (arrive_safe // blocks_x - group_at * LB_DEV) * BX_SEG + (
        arrive_safe % blocks_x - pencil_at * BX_SEG
    )
    local_block = jnp.where(arrive_live, local_block, BPD).astype(jnp.int32)
    which_arrived = (
        jnp.full((BPD,), n_arrived, jnp.int32)
        .at[local_block]
        .set(jnp.arange(n_arrived, dtype=jnp.int32), mode="drop")
    )
    block_active = (which_arrived < n_arrived).astype(jnp.float32)
    tile_flow = jnp.take(got_flow, which_arrived, axis=0, mode="fill", fill_value=0.0)
    tile_visc = jnp.take(got_visc, which_arrived, axis=0, mode="fill", fill_value=0.0)
    tile_mass = jnp.take(got_mass, which_arrived, axis=0, mode="fill", fill_value=0.0)
    flow_grid = (
        tile_flow.reshape(LB_DEV, BX_SEG, 3, EDGE, edge_sq)
        .transpose(2, 1, 3, 0, 4)
        .reshape(3, seg_width, lines_here)
    )
    visc_grid = (
        tile_visc.reshape(LB_DEV, BX_SEG, EDGE, edge_sq)
        .transpose(1, 2, 0, 3)
        .reshape(seg_width, lines_here)
    )
    mass_grid = (
        tile_mass.reshape(LB_DEV, BX_SEG, EDGE, edge_sq)
        .transpose(1, 2, 0, 3)
        .reshape(seg_width, lines_here)
    )
    active = jnp.broadcast_to(
        block_active.reshape(LB_DEV, BX_SEG).T[:, None, :, None], (BX_SEG, EDGE, LB_DEV, edge_sq)
    ).reshape(seg_width, lines_here)
    rimmed = padded(jnp.stack([visc_grid, active], axis=0), (("pencil", 1),), 1)
    face_visc = 0.5 * (rimmed[0, :-1] + rimmed[0, 1:]) * rimmed[1, :-1] * rimmed[1, 1:]
    face_left = face_visc[:-1]
    face_right = face_visc[1:]
    lower_band = -face_left
    upper_band = -face_right
    main_band = mass_grid + face_left + face_right + (1.0 - active)
    right_side = mass_grid[None] * flow_grid
    prev_lower = -jnp.ones((lines_here,), jnp.float32)
    prev_upper = jnp.zeros((lines_here,), jnp.float32)
    prev_right = jnp.zeros((3, lines_here), jnp.float32)
    fwd_lower, fwd_upper, fwd_right = ([], [], [])
    for cell_x in range(1, seg_width):
        low_coef = lower_band[cell_x]
        pivot_inv = 1.0 / (main_band[cell_x] - low_coef * prev_upper)
        prev_lower = -low_coef * prev_lower * pivot_inv
        prev_upper = upper_band[cell_x] * pivot_inv
        prev_right = (right_side[:, cell_x] - low_coef[None, :] * prev_right) * pivot_inv[None, :]
        fwd_lower.append(prev_lower)
        fwd_upper.append(prev_upper)
        fwd_right.append(prev_right)
    next_lower = jnp.zeros((lines_here,), jnp.float32)
    next_upper = -jnp.ones((lines_here,), jnp.float32)
    next_right = jnp.zeros((3, lines_here), jnp.float32)
    back_lower = [None] * (seg_width - 2)
    back_upper = [None] * (seg_width - 2)
    back_right = [None] * (seg_width - 2)
    for index_k in range(seg_width - 3, -1, -1):
        row_upper = fwd_upper[index_k]
        next_right = fwd_right[index_k] - row_upper[None, :] * next_right
        next_lower = fwd_lower[index_k] - row_upper * next_lower
        next_upper = -row_upper * next_upper
        back_lower[index_k] = next_lower
        back_upper[index_k] = next_upper
        back_right[index_k] = next_right
    first_row = jnp.concatenate(
        [
            lower_band[0][None],
            (main_band[0] - upper_band[0] * back_lower[0])[None],
            (-upper_band[0] * back_upper[0])[None],
            right_side[:, 0] - upper_band[0][None, :] * back_right[0],
        ],
        axis=0,
    )
    last_row = jnp.concatenate(
        [
            fwd_lower[-1][None],
            jnp.ones((1, lines_here), jnp.float32),
            fwd_upper[-1][None],
            fwd_right[-1],
        ],
        axis=0,
    )
    reduced = jnp.stack([first_row, last_row])
    chunk = lines_here // n_pencil
    sent_rows = reduced.reshape(2, 6, n_pencil, chunk).transpose(2, 0, 1, 3)
    all_rows = lax.all_to_all(sent_rows, "pencil", 0, 0, tiled=True)
    all_rows = all_rows.reshape(2 * n_pencil, 6, chunk)
    scaled_upper = []
    scaled_right = []
    carry_upper = jnp.zeros((chunk,), jnp.float32)
    carry_right = jnp.zeros((3, chunk), jnp.float32)
    for row_at in range(2 * n_pencil):
        row_lower = all_rows[row_at, 0]
        row_inv = 1.0 / (all_rows[row_at, 1] - row_lower * carry_upper)
        carry_upper = all_rows[row_at, 2] * row_inv
        carry_right = (all_rows[row_at, 3:] - row_lower[None, :] * carry_right) * row_inv[None, :]
        scaled_upper.append(carry_upper)
        scaled_right.append(carry_right)
    ends = [None] * (2 * n_pencil)
    ends[-1] = scaled_right[-1]
    for row_at in range(2 * n_pencil - 2, -1, -1):
        ends[row_at] = scaled_right[row_at] - scaled_upper[row_at][None, :] * ends[row_at + 1]
    solved_ends = jnp.stack(ends).reshape(n_pencil, 2, 3, chunk)
    solved_ends = lax.all_to_all(solved_ends, "pencil", 0, 0, tiled=True)
    solution_ends = solved_ends.transpose(1, 2, 0, 3).reshape(2, 3, lines_here)
    end_first = solution_ends[0]
    end_last = solution_ends[1]
    columns = [end_first]
    for index_k in range(seg_width - 2):
        columns.append(
            back_right[index_k]
            - back_lower[index_k][None, :] * end_first
            - back_upper[index_k][None, :] * end_last
        )
    columns.append(end_last)
    return jnp.stack(columns, axis=1)


def solution(mesh):
    in_specs = (
        P(("pencil", "group"), None, None),
        P(("pencil", "group"), None),
        P(("pencil", "group"), None),
        P(("pencil", "group")),
    )
    out_specs = P(None, "pencil", "group")
    return jax.shard_map(
        on_device, mesh=mesh, in_specs=in_specs, out_specs=out_specs, check_vma=False
    )
```

```python
import jax
import jax.numpy as jnp
from jax import lax
from jax.sharding import PartitionSpec as P

EDGE = 8
CELLS = 512
BX_SEG = 3
LB_DEV = 128
BPD = 384


def shifted(value, axis, steps):
    count = lax.axis_size(axis)
    first, last = (max(0, -steps), min(count, count - steps))
    return lax.ppermute(value, axis, [(source, source + steps) for source in range(first, last)])


def padded(block, sides, width):
    for axis, dim in sides:
        count = lax.axis_size(axis)
        forward = [(i, i + 1) for i in range(count - 1)]
        backward = [(target, source) for source, target in forward]
        low = lax.ppermute(
            lax.slice_in_dim(block, block.shape[dim] - width, None, axis=dim), axis, forward
        )
        high = lax.ppermute(lax.slice_in_dim(block, 0, width, axis=dim), axis, backward)
        block = jnp.concatenate([low, block, high], axis=dim)
    return block


def combine_rows(row_set, before, after_rows, left_ok, right_ok):
    alpha = jnp.where(
        left_ok, -row_set[..., 0, :] / jnp.where(left_ok, before[..., 1, :], 1.0), 0.0
    )
    gamma = jnp.where(
        right_ok, -row_set[..., 2, :] / jnp.where(right_ok, after_rows[..., 1, :], 1.0), 0.0
    )
    new_lower = alpha * before[..., 0, :]
    new_upper = gamma * after_rows[..., 2, :]
    new_main = row_set[..., 1, :] + alpha * before[..., 2, :] + gamma * after_rows[..., 0, :]
    new_right = (
        row_set[..., 3:, :]
        + alpha[..., None, :] * before[..., 3:, :]
        + gamma[..., None, :] * after_rows[..., 3:, :]
    )
    return jnp.concatenate(
        [new_lower[..., None, :], new_main[..., None, :], new_upper[..., None, :], new_right],
        axis=-2,
    )


def neighbours(left_part, right_part, offset):
    from_left = shifted(left_part, "pencil", offset)
    from_right = shifted(right_part, "pencil", -offset)
    return (from_left, from_right)


def on_device(velocity, viscosity, density, slot_block):
    n_pencil = lax.axis_size("pencil")
    n_group = lax.axis_size("group")
    devices = n_pencil * n_group
    n_slots = slot_block.shape[0]
    capacity = n_slots // devices
    blocks_x = BX_SEG * n_pencil
    edge_sq = EDGE * EDGE
    seg_width = EDGE * BX_SEG
    lines_here = LB_DEV * edge_sq
    live_slot = slot_block >= 0
    safe_ids = jnp.where(live_slot, slot_block, 0)
    block_x = safe_ids % blocks_x
    block_line = safe_ids // blocks_x
    target = block_x // BX_SEG * n_group + block_line // LB_DEV
    one_hot = jnp.logical_and(
        target[:, None] == jnp.arange(devices, dtype=jnp.int32)[None, :], live_slot[:, None]
    ).astype(jnp.int32)
    target_rank = jnp.sum((jnp.cumsum(one_hot, axis=0) - 1) * one_hot, axis=1)
    position = jnp.where(live_slot, target * capacity + target_rank, devices * capacity)
    source_of = (
        jnp.full((devices * capacity,), n_slots, jnp.int32)
        .at[position]
        .set(jnp.arange(n_slots, dtype=jnp.int32), mode="drop")
    )
    send_flow = jnp.take(velocity, source_of, axis=0, mode="fill", fill_value=0.0)
    send_visc = jnp.take(viscosity, source_of, axis=0, mode="fill", fill_value=0.0)
    send_mass = jnp.take(density, source_of, axis=0, mode="fill", fill_value=0.0)
    labels = jnp.take(slot_block, source_of, axis=0, mode="fill", fill_value=-1)
    def exchange(value):
        return lax.all_to_all(
            value.reshape((devices, capacity) + value.shape[1:]),
            ("pencil", "group"),
            split_axis=0,
            concat_axis=0,
            tiled=True,
        )

    arrived_ids = exchange(labels)
    arrived_ids, send_flow = lax.optimization_barrier((arrived_ids, send_flow))
    got_flow = exchange(send_flow)
    got_flow, send_visc = lax.optimization_barrier((got_flow, send_visc))
    got_visc = exchange(send_visc)
    got_visc, send_mass = lax.optimization_barrier((got_visc, send_mass))
    got_mass = exchange(send_mass)
    n_arrived = devices * capacity
    got_flow = got_flow.reshape(n_arrived, 3, CELLS)
    got_visc = got_visc.reshape(n_arrived, CELLS)
    got_mass = got_mass.reshape(n_arrived, CELLS)
    arrived_ids = arrived_ids.reshape(n_arrived)
    pencil_at = lax.axis_index("pencil")
    group_at = lax.axis_index("group")
    arrive_live = arrived_ids >= 0
    arrive_safe = jnp.where(arrive_live, arrived_ids, 0)
    local_block = (arrive_safe // blocks_x - group_at * LB_DEV) * BX_SEG + (
        arrive_safe % blocks_x - pencil_at * BX_SEG
    )
    local_block = jnp.where(arrive_live, local_block, BPD).astype(jnp.int32)
    which_arrived = (
        jnp.full((BPD,), n_arrived, jnp.int32)
        .at[local_block]
        .set(jnp.arange(n_arrived, dtype=jnp.int32), mode="drop")
    )
    block_active = (which_arrived < n_arrived).astype(jnp.float32)
    tile_flow = jnp.take(got_flow, which_arrived, axis=0, mode="fill", fill_value=0.0)
    tile_visc = jnp.take(got_visc, which_arrived, axis=0, mode="fill", fill_value=0.0)
    tile_mass = jnp.take(got_mass, which_arrived, axis=0, mode="fill", fill_value=0.0)
    flow_grid = (
        tile_flow.reshape(LB_DEV, BX_SEG, 3, EDGE, edge_sq)
        .transpose(2, 1, 3, 0, 4)
        .reshape(3, seg_width, lines_here)
    )
    visc_grid = (
        tile_visc.reshape(LB_DEV, BX_SEG, EDGE, edge_sq)
        .transpose(1, 2, 0, 3)
        .reshape(seg_width, lines_here)
    )
    mass_grid = (
        tile_mass.reshape(LB_DEV, BX_SEG, EDGE, edge_sq)
        .transpose(1, 2, 0, 3)
        .reshape(seg_width, lines_here)
    )
    active = jnp.broadcast_to(
        block_active.reshape(LB_DEV, BX_SEG).T[:, None, :, None], (BX_SEG, EDGE, LB_DEV, edge_sq)
    ).reshape(seg_width, lines_here)
    rimmed = padded(jnp.stack([visc_grid, active], axis=0), (("pencil", 1),), 1)
    face_visc = 0.5 * (rimmed[0, :-1] + rimmed[0, 1:]) * rimmed[1, :-1] * rimmed[1, 1:]
    face_left = face_visc[:-1]
    face_right = face_visc[1:]
    lower_band = -face_left
    upper_band = -face_right
    main_band = mass_grid + face_left + face_right + (1.0 - active)
    right_side = mass_grid[None] * flow_grid
    prev_lower = -jnp.ones((lines_here,), jnp.float32)
    prev_upper = jnp.zeros((lines_here,), jnp.float32)
    prev_right = jnp.zeros((3, lines_here), jnp.float32)
    fwd_lower, fwd_upper, fwd_right = ([], [], [])
    for cell_x in range(1, seg_width):
        low_coef = lower_band[cell_x]
        pivot_inv = 1.0 / (main_band[cell_x] - low_coef * prev_upper)
        prev_lower = -low_coef * prev_lower * pivot_inv
        prev_upper = upper_band[cell_x] * pivot_inv
        prev_right = (right_side[:, cell_x] - low_coef[None, :] * prev_right) * pivot_inv[None, :]
        fwd_lower.append(prev_lower)
        fwd_upper.append(prev_upper)
        fwd_right.append(prev_right)
    next_lower = jnp.zeros((lines_here,), jnp.float32)
    next_upper = -jnp.ones((lines_here,), jnp.float32)
    next_right = jnp.zeros((3, lines_here), jnp.float32)
    back_lower = [None] * (seg_width - 2)
    back_upper = [None] * (seg_width - 2)
    back_right = [None] * (seg_width - 2)
    for index_k in range(seg_width - 3, -1, -1):
        row_upper = fwd_upper[index_k]
        next_right = fwd_right[index_k] - row_upper[None, :] * next_right
        next_lower = fwd_lower[index_k] - row_upper * next_lower
        next_upper = -row_upper * next_upper
        back_lower[index_k] = next_lower
        back_upper[index_k] = next_upper
        back_right[index_k] = next_right
    first_row = jnp.concatenate(
        [
            lower_band[0][None],
            (main_band[0] - upper_band[0] * back_lower[0])[None],
            (-upper_band[0] * back_upper[0])[None],
            right_side[:, 0] - upper_band[0][None, :] * back_right[0],
        ],
        axis=0,
    )
    last_row = jnp.concatenate(
        [
            fwd_lower[-1][None],
            jnp.ones((1, lines_here), jnp.float32),
            fwd_upper[-1][None],
            fwd_right[-1],
        ],
        axis=0,
    )
    reduced = jnp.stack([first_row, last_row])
    chunk = lines_here // n_pencil
    sent_rows = reduced.reshape(2, 6, n_pencil, chunk).transpose(2, 0, 1, 3)
    all_rows = lax.all_to_all(sent_rows, "pencil", 0, 0, tiled=True)
    all_rows = all_rows.reshape(2 * n_pencil, 6, chunk)
    scaled_upper = []
    scaled_right = []
    carry_upper = jnp.zeros((chunk,), jnp.float32)
    carry_right = jnp.zeros((3, chunk), jnp.float32)
    for row_at in range(2 * n_pencil):
        row_lower = all_rows[row_at, 0]
        row_inv = 1.0 / (all_rows[row_at, 1] - row_lower * carry_upper)
        carry_upper = all_rows[row_at, 2] * row_inv
        carry_right = (all_rows[row_at, 3:] - row_lower[None, :] * carry_right) * row_inv[None, :]
        scaled_upper.append(carry_upper)
        scaled_right.append(carry_right)
    ends = [None] * (2 * n_pencil)
    ends[-1] = scaled_right[-1]
    for row_at in range(2 * n_pencil - 2, -1, -1):
        ends[row_at] = scaled_right[row_at] - scaled_upper[row_at][None, :] * ends[row_at + 1]
    solved_ends = jnp.stack(ends).reshape(n_pencil, 2, 3, chunk)
    solved_ends = lax.all_to_all(solved_ends, "pencil", 0, 0, tiled=True)
    solution_ends = solved_ends.transpose(1, 2, 0, 3).reshape(2, 3, lines_here)
    end_first = solution_ends[0]
    end_last = solution_ends[1]
    columns = [end_first]
    for index_k in range(seg_width - 2):
        columns.append(
            back_right[index_k]
            - back_lower[index_k][None, :] * end_first
            - back_upper[index_k][None, :] * end_last
        )
    columns.append(end_last)
    return jnp.stack(columns, axis=1)


def solution(mesh):
    in_specs = (
        P(("pencil", "group"), None, None),
        P(("pencil", "group"), None),
        P(("pencil", "group"), None),
        P(("pencil", "group")),
    )
    out_specs = P(None, "pencil", "group")
    return jax.shard_map(
        on_device, mesh=mesh, in_specs=in_specs, out_specs=out_specs, check_vma=False
    )
```

```python
import jax
import jax.numpy as jnp
from jax import lax
from jax.sharding import PartitionSpec as P

EDGE = 8
CELLS = 512
BX_SEG = 3
LB_DEV = 128
BPD = 384


def shifted(value, axis, steps):
    count = lax.axis_size(axis)
    first, last = (max(0, -steps), min(count, count - steps))
    return lax.ppermute(value, axis, [(source, source + steps) for source in range(first, last)])


def padded(block, sides, width):
    for axis, dim in sides:
        count = lax.axis_size(axis)
        forward = [(i, i + 1) for i in range(count - 1)]
        backward = [(target, source) for source, target in forward]
        low = lax.ppermute(
            lax.slice_in_dim(block, block.shape[dim] - width, None, axis=dim), axis, forward
        )
        high = lax.ppermute(lax.slice_in_dim(block, 0, width, axis=dim), axis, backward)
        block = jnp.concatenate([low, block, high], axis=dim)
    return block


def combine_rows(row_set, before, after_rows, left_ok, right_ok):
    alpha = jnp.where(
        left_ok, -row_set[..., 0, :] / jnp.where(left_ok, before[..., 1, :], 1.0), 0.0
    )
    gamma = jnp.where(
        right_ok, -row_set[..., 2, :] / jnp.where(right_ok, after_rows[..., 1, :], 1.0), 0.0
    )
    new_lower = alpha * before[..., 0, :]
    new_upper = gamma * after_rows[..., 2, :]
    new_main = row_set[..., 1, :] + alpha * before[..., 2, :] + gamma * after_rows[..., 0, :]
    new_right = (
        row_set[..., 3:, :]
        + alpha[..., None, :] * before[..., 3:, :]
        + gamma[..., None, :] * after_rows[..., 3:, :]
    )
    return jnp.concatenate(
        [new_lower[..., None, :], new_main[..., None, :], new_upper[..., None, :], new_right],
        axis=-2,
    )


def neighbours(left_part, right_part, offset):
    from_left = shifted(left_part, "pencil", offset)
    from_right = shifted(right_part, "pencil", -offset)
    return (from_left, from_right)


def on_device(velocity, viscosity, density, slot_block):
    n_pencil = lax.axis_size("pencil")
    n_group = lax.axis_size("group")
    devices = n_pencil * n_group
    n_slots = slot_block.shape[0]
    capacity = n_slots // devices
    blocks_x = BX_SEG * n_pencil
    edge_sq = EDGE * EDGE
    seg_width = EDGE * BX_SEG
    lines_here = LB_DEV * edge_sq
    live_slot = slot_block >= 0
    safe_ids = jnp.where(live_slot, slot_block, 0)
    block_x = safe_ids % blocks_x
    block_line = safe_ids // blocks_x
    target = block_x // BX_SEG * n_group + block_line // LB_DEV
    one_hot = jnp.logical_and(
        target[:, None] == jnp.arange(devices, dtype=jnp.int32)[None, :], live_slot[:, None]
    ).astype(jnp.int32)
    target_rank = jnp.sum((jnp.cumsum(one_hot, axis=0) - 1) * one_hot, axis=1)
    position = jnp.where(live_slot, target * capacity + target_rank, devices * capacity)
    source_of = (
        jnp.full((devices * capacity,), n_slots, jnp.int32)
        .at[position]
        .set(jnp.arange(n_slots, dtype=jnp.int32), mode="drop")
    )
    width = 5 * CELLS
    fields = jnp.concatenate(
        [velocity, viscosity[:, None, :], density[:, None, :]], axis=1
    ).reshape(n_slots, width)
    labels = jnp.take(slot_block, source_of, axis=0, mode="fill", fill_value=-1)
    arrived_ids = lax.all_to_all(
        labels.reshape(devices, capacity),
        ("pencil", "group"),
        split_axis=0,
        concat_axis=0,
        tiled=True,
    )
    send_all = jnp.take(fields, source_of, axis=0, mode="fill", fill_value=0.0)
    arrived_ids, send_all = lax.optimization_barrier((arrived_ids, send_all))
    got_all = lax.all_to_all(
        send_all.reshape(devices, capacity, width),
        ("pencil", "group"),
        split_axis=0,
        concat_axis=0,
        tiled=True,
    )
    n_arrived = devices * capacity
    got_all = got_all.reshape(n_arrived, width)
    arrived_ids = arrived_ids.reshape(n_arrived)
    pencil_at = lax.axis_index("pencil")
    group_at = lax.axis_index("group")
    arrive_live = arrived_ids >= 0
    arrive_safe = jnp.where(arrive_live, arrived_ids, 0)
    local_block = (arrive_safe // blocks_x - group_at * LB_DEV) * BX_SEG + (
        arrive_safe % blocks_x - pencil_at * BX_SEG
    )
    local_block = jnp.where(arrive_live, local_block, BPD).astype(jnp.int32)
    which_arrived = (
        jnp.full((BPD,), n_arrived, jnp.int32)
        .at[local_block]
        .set(jnp.arange(n_arrived, dtype=jnp.int32), mode="drop")
    )
    block_active = (which_arrived < n_arrived).astype(jnp.float32)
    tiles = jnp.take(got_all, which_arrived, axis=0, mode="fill", fill_value=0.0)
    grid = (
        tiles.reshape(LB_DEV, BX_SEG, 5, EDGE, edge_sq)
        .transpose(2, 1, 3, 0, 4)
        .reshape(5, seg_width, lines_here)
    )
    flow_grid = grid[:3]
    visc_grid = grid[3]
    mass_grid = grid[4]
    active = jnp.broadcast_to(
        block_active.reshape(LB_DEV, BX_SEG).T[:, None, :, None], (BX_SEG, EDGE, LB_DEV, edge_sq)
    ).reshape(seg_width, lines_here)
    rimmed = padded(jnp.stack([visc_grid, active], axis=0), (("pencil", 1),), 1)
    face_visc = 0.5 * (rimmed[0, :-1] + rimmed[0, 1:]) * rimmed[1, :-1] * rimmed[1, 1:]
    face_left = face_visc[:-1]
    face_right = face_visc[1:]
    lower_band = -face_left
    upper_band = -face_right
    main_band = mass_grid + face_left + face_right + (1.0 - active)
    right_side = mass_grid[None] * flow_grid
    prev_lower = -jnp.ones((lines_here,), jnp.float32)
    prev_upper = jnp.zeros((lines_here,), jnp.float32)
    prev_right = jnp.zeros((3, lines_here), jnp.float32)
    fwd_lower, fwd_upper, fwd_right = ([], [], [])
    for cell_x in range(1, seg_width):
        low_coef = lower_band[cell_x]
        pivot_inv = 1.0 / (main_band[cell_x] - low_coef * prev_upper)
        prev_lower = -low_coef * prev_lower * pivot_inv
        prev_upper = upper_band[cell_x] * pivot_inv
        prev_right = (right_side[:, cell_x] - low_coef[None, :] * prev_right) * pivot_inv[None, :]
        fwd_lower.append(prev_lower)
        fwd_upper.append(prev_upper)
        fwd_right.append(prev_right)
    next_lower = jnp.zeros((lines_here,), jnp.float32)
    next_upper = -jnp.ones((lines_here,), jnp.float32)
    next_right = jnp.zeros((3, lines_here), jnp.float32)
    back_lower = [None] * (seg_width - 2)
    back_upper = [None] * (seg_width - 2)
    back_right = [None] * (seg_width - 2)
    for index_k in range(seg_width - 3, -1, -1):
        row_upper = fwd_upper[index_k]
        next_right = fwd_right[index_k] - row_upper[None, :] * next_right
        next_lower = fwd_lower[index_k] - row_upper * next_lower
        next_upper = -row_upper * next_upper
        back_lower[index_k] = next_lower
        back_upper[index_k] = next_upper
        back_right[index_k] = next_right
    first_row = jnp.concatenate(
        [
            lower_band[0][None],
            (main_band[0] - upper_band[0] * back_lower[0])[None],
            (-upper_band[0] * back_upper[0])[None],
            right_side[:, 0] - upper_band[0][None, :] * back_right[0],
        ],
        axis=0,
    )
    last_row = jnp.concatenate(
        [
            fwd_lower[-1][None],
            jnp.ones((1, lines_here), jnp.float32),
            fwd_upper[-1][None],
            fwd_right[-1],
        ],
        axis=0,
    )
    reduced = jnp.stack([first_row, last_row])
    chunk = lines_here // n_pencil
    sent_rows = reduced.reshape(2, 6, n_pencil, chunk).transpose(2, 0, 1, 3)
    all_rows = lax.all_to_all(sent_rows, "pencil", 0, 0, tiled=True)
    all_rows = all_rows.reshape(2 * n_pencil, 6, chunk)
    scaled_upper = []
    scaled_right = []
    carry_upper = jnp.zeros((chunk,), jnp.float32)
    carry_right = jnp.zeros((3, chunk), jnp.float32)
    for row_at in range(2 * n_pencil):
        row_lower = all_rows[row_at, 0]
        row_inv = 1.0 / (all_rows[row_at, 1] - row_lower * carry_upper)
        carry_upper = all_rows[row_at, 2] * row_inv
        carry_right = (all_rows[row_at, 3:] - row_lower[None, :] * carry_right) * row_inv[None, :]
        scaled_upper.append(carry_upper)
        scaled_right.append(carry_right)
    ends = [None] * (2 * n_pencil)
    ends[-1] = scaled_right[-1]
    for row_at in range(2 * n_pencil - 2, -1, -1):
        ends[row_at] = scaled_right[row_at] - scaled_upper[row_at][None, :] * ends[row_at + 1]
    solved_ends = jnp.stack(ends).reshape(n_pencil, 2, 3, chunk)
    solved_ends = lax.all_to_all(solved_ends, "pencil", 0, 0, tiled=True)
    solution_ends = solved_ends.transpose(1, 2, 0, 3).reshape(2, 3, lines_here)
    end_first = solution_ends[0]
    end_last = solution_ends[1]
    columns = [end_first]
    for index_k in range(seg_width - 2):
        columns.append(
            back_right[index_k]
            - back_lower[index_k][None, :] * end_first
            - back_upper[index_k][None, :] * end_last
        )
    columns.append(end_last)
    return jnp.stack(columns, axis=1)


def solution(mesh):
    in_specs = (
        P(("pencil", "group"), None, None),
        P(("pencil", "group"), None),
        P(("pencil", "group"), None),
        P(("pencil", "group")),
    )
    out_specs = P(None, "pencil", "group")
    return jax.shard_map(
        on_device, mesh=mesh, in_specs=in_specs, out_specs=out_specs, check_vma=False
    )
```

```python
import jax
import jax.numpy as jnp
from jax import lax
from jax.sharding import PartitionSpec as P

EDGE = 8
CELLS = 512
BX_SEG = 3
LB_DEV = 128
BPD = 384


def shifted(value, axis, steps):
    count = lax.axis_size(axis)
    first, last = (max(0, -steps), min(count, count - steps))
    return lax.ppermute(value, axis, [(source, source + steps) for source in range(first, last)])


def padded(block, sides, width):
    for axis, dim in sides:
        count = lax.axis_size(axis)
        forward = [(i, i + 1) for i in range(count - 1)]
        backward = [(target, source) for source, target in forward]
        low = lax.ppermute(
            lax.slice_in_dim(block, block.shape[dim] - width, None, axis=dim), axis, forward
        )
        high = lax.ppermute(lax.slice_in_dim(block, 0, width, axis=dim), axis, backward)
        block = jnp.concatenate([low, block, high], axis=dim)
    return block


def combine_rows(row_set, before, after_rows, left_ok, right_ok):
    alpha = jnp.where(
        left_ok, -row_set[..., 0, :] / jnp.where(left_ok, before[..., 1, :], 1.0), 0.0
    )
    gamma = jnp.where(
        right_ok, -row_set[..., 2, :] / jnp.where(right_ok, after_rows[..., 1, :], 1.0), 0.0
    )
    new_lower = alpha * before[..., 0, :]
    new_upper = gamma * after_rows[..., 2, :]
    new_main = row_set[..., 1, :] + alpha * before[..., 2, :] + gamma * after_rows[..., 0, :]
    new_right = (
        row_set[..., 3:, :]
        + alpha[..., None, :] * before[..., 3:, :]
        + gamma[..., None, :] * after_rows[..., 3:, :]
    )
    return jnp.concatenate(
        [new_lower[..., None, :], new_main[..., None, :], new_upper[..., None, :], new_right],
        axis=-2,
    )


def neighbours(left_part, right_part, offset):
    from_left = shifted(left_part, "pencil", offset)
    from_right = shifted(right_part, "pencil", -offset)
    return (from_left, from_right)


def on_device(velocity, viscosity, density, slot_block):
    n_pencil = lax.axis_size("pencil")
    n_group = lax.axis_size("group")
    devices = n_pencil * n_group
    n_slots = slot_block.shape[0]
    capacity = n_slots // devices
    blocks_x = BX_SEG * n_pencil
    edge_sq = EDGE * EDGE
    seg_width = EDGE * BX_SEG
    lines_here = LB_DEV * edge_sq
    live_slot = slot_block >= 0
    safe_ids = jnp.where(live_slot, slot_block, 0)
    block_x = safe_ids % blocks_x
    block_line = safe_ids // blocks_x
    target = block_x // BX_SEG * n_group + block_line // LB_DEV
    one_hot = jnp.logical_and(
        target[:, None] == jnp.arange(devices, dtype=jnp.int32)[None, :], live_slot[:, None]
    ).astype(jnp.int32)
    target_rank = jnp.sum((jnp.cumsum(one_hot, axis=0) - 1) * one_hot, axis=1)
    position = jnp.where(live_slot, target * capacity + target_rank, devices * capacity)
    source_of = (
        jnp.full((devices * capacity,), n_slots, jnp.int32)
        .at[position]
        .set(jnp.arange(n_slots, dtype=jnp.int32), mode="drop")
    )
    send_flow = jnp.take(velocity, source_of, axis=0, mode="clip")
    send_visc = jnp.take(viscosity, source_of, axis=0, mode="clip")
    send_mass = jnp.take(density, source_of, axis=0, mode="clip")
    labels = jnp.take(slot_block, source_of, axis=0, mode="fill", fill_value=-1)
    got_flow, got_visc, got_mass, arrived_ids = (
        lax.all_to_all(
            send_flow.reshape(devices, capacity, 3, CELLS),
            ("pencil", "group"),
            split_axis=0,
            concat_axis=0,
            tiled=True,
        ),
        lax.all_to_all(
            send_visc.reshape(devices, capacity, CELLS),
            ("pencil", "group"),
            split_axis=0,
            concat_axis=0,
            tiled=True,
        ),
        lax.all_to_all(
            send_mass.reshape(devices, capacity, CELLS),
            ("pencil", "group"),
            split_axis=0,
            concat_axis=0,
            tiled=True,
        ),
        lax.all_to_all(
            labels.reshape(devices, capacity),
            ("pencil", "group"),
            split_axis=0,
            concat_axis=0,
            tiled=True,
        ),
    )
    n_arrived = devices * capacity
    got_flow = got_flow.reshape(n_arrived, 3, CELLS)
    got_visc = got_visc.reshape(n_arrived, CELLS)
    got_mass = got_mass.reshape(n_arrived, CELLS)
    arrived_ids = arrived_ids.reshape(n_arrived)
    pencil_at = lax.axis_index("pencil")
    group_at = lax.axis_index("group")
    arrive_live = arrived_ids >= 0
    arrive_safe = jnp.where(arrive_live, arrived_ids, 0)
    local_block = (arrive_safe // blocks_x - group_at * LB_DEV) * BX_SEG + (
        arrive_safe % blocks_x - pencil_at * BX_SEG
    )
    local_block = jnp.where(arrive_live, local_block, BPD).astype(jnp.int32)
    which_arrived = (
        jnp.full((BPD,), n_arrived, jnp.int32)
        .at[local_block]
        .set(jnp.arange(n_arrived, dtype=jnp.int32), mode="drop")
    )
    block_active = (which_arrived < n_arrived).astype(jnp.float32)
    tile_flow = jnp.take(got_flow, which_arrived, axis=0, mode="clip")
    tile_visc = jnp.take(got_visc, which_arrived, axis=0, mode="clip")
    tile_mass = jnp.take(got_mass, which_arrived, axis=0, mode="fill", fill_value=0.0)
    flow_grid = (
        tile_flow.reshape(LB_DEV, BX_SEG, 3, EDGE, edge_sq)
        .transpose(2, 1, 3, 0, 4)
        .reshape(3, seg_width, lines_here)
    )
    visc_grid = (
        tile_visc.reshape(LB_DEV, BX_SEG, EDGE, edge_sq)
        .transpose(1, 2, 0, 3)
        .reshape(seg_width, lines_here)
    )
    mass_grid = (
        tile_mass.reshape(LB_DEV, BX_SEG, EDGE, edge_sq)
        .transpose(1, 2, 0, 3)
        .reshape(seg_width, lines_here)
    )
    active = jnp.broadcast_to(
        block_active.reshape(LB_DEV, BX_SEG).T[:, None, :, None], (BX_SEG, EDGE, LB_DEV, edge_sq)
    ).reshape(seg_width, lines_here)
    rimmed = padded(jnp.stack([visc_grid, active], axis=0), (("pencil", 1),), 1)
    face_visc = 0.5 * (rimmed[0, :-1] + rimmed[0, 1:]) * rimmed[1, :-1] * rimmed[1, 1:]
    face_left = face_visc[:-1]
    face_right = face_visc[1:]
    lower_band = -face_left
    upper_band = -face_right
    main_band = mass_grid + face_left + face_right + (1.0 - active)
    right_side = mass_grid[None] * flow_grid
    prev_lower = -jnp.ones((lines_here,), jnp.float32)
    prev_upper = jnp.zeros((lines_here,), jnp.float32)
    prev_right = jnp.zeros((3, lines_here), jnp.float32)
    fwd_lower, fwd_upper, fwd_right = ([], [], [])
    for cell_x in range(1, seg_width):
        low_coef = lower_band[cell_x]
        pivot_inv = 1.0 / (main_band[cell_x] - low_coef * prev_upper)
        prev_lower = -low_coef * prev_lower * pivot_inv
        prev_upper = upper_band[cell_x] * pivot_inv
        prev_right = (right_side[:, cell_x] - low_coef[None, :] * prev_right) * pivot_inv[None, :]
        fwd_lower.append(prev_lower)
        fwd_upper.append(prev_upper)
        fwd_right.append(prev_right)
    next_lower = jnp.zeros((lines_here,), jnp.float32)
    next_upper = -jnp.ones((lines_here,), jnp.float32)
    next_right = jnp.zeros((3, lines_here), jnp.float32)
    back_lower = [None] * (seg_width - 2)
    back_upper = [None] * (seg_width - 2)
    back_right = [None] * (seg_width - 2)
    for index_k in range(seg_width - 3, -1, -1):
        row_upper = fwd_upper[index_k]
        next_right = fwd_right[index_k] - row_upper[None, :] * next_right
        next_lower = fwd_lower[index_k] - row_upper * next_lower
        next_upper = -row_upper * next_upper
        back_lower[index_k] = next_lower
        back_upper[index_k] = next_upper
        back_right[index_k] = next_right
    first_row = jnp.concatenate(
        [
            lower_band[0][None],
            (main_band[0] - upper_band[0] * back_lower[0])[None],
            (-upper_band[0] * back_upper[0])[None],
            right_side[:, 0] - upper_band[0][None, :] * back_right[0],
        ],
        axis=0,
    )
    last_row = jnp.concatenate(
        [
            fwd_lower[-1][None],
            jnp.ones((1, lines_here), jnp.float32),
            fwd_upper[-1][None],
            fwd_right[-1],
        ],
        axis=0,
    )
    reduced = jnp.stack([first_row, last_row])
    chunk = lines_here // n_pencil
    sent_rows = reduced.reshape(2, 6, n_pencil, chunk).transpose(2, 0, 1, 3)
    all_rows = lax.all_to_all(sent_rows, "pencil", 0, 0, tiled=True)
    all_rows = all_rows.reshape(2 * n_pencil, 6, chunk)
    scaled_upper = []
    scaled_right = []
    carry_upper = jnp.zeros((chunk,), jnp.float32)
    carry_right = jnp.zeros((3, chunk), jnp.float32)
    for row_at in range(2 * n_pencil):
        row_lower = all_rows[row_at, 0]
        row_inv = 1.0 / (all_rows[row_at, 1] - row_lower * carry_upper)
        carry_upper = all_rows[row_at, 2] * row_inv
        carry_right = (all_rows[row_at, 3:] - row_lower[None, :] * carry_right) * row_inv[None, :]
        scaled_upper.append(carry_upper)
        scaled_right.append(carry_right)
    ends = [None] * (2 * n_pencil)
    ends[-1] = scaled_right[-1]
    for row_at in range(2 * n_pencil - 2, -1, -1):
        ends[row_at] = scaled_right[row_at] - scaled_upper[row_at][None, :] * ends[row_at + 1]
    solved_ends = jnp.stack(ends).reshape(n_pencil, 2, 3, chunk)
    solved_ends = lax.all_to_all(solved_ends, "pencil", 0, 0, tiled=True)
    solution_ends = solved_ends.transpose(1, 2, 0, 3).reshape(2, 3, lines_here)
    end_first = solution_ends[0]
    end_last = solution_ends[1]
    columns = [end_first]
    for index_k in range(seg_width - 2):
        columns.append(
            back_right[index_k]
            - back_lower[index_k][None, :] * end_first
            - back_upper[index_k][None, :] * end_last
        )
    columns.append(end_last)
    return jnp.stack(columns, axis=1)


def solution(mesh):
    in_specs = (
        P(("pencil", "group"), None, None),
        P(("pencil", "group"), None),
        P(("pencil", "group"), None),
        P(("pencil", "group")),
    )
    out_specs = P(None, "pencil", "group")
    return jax.shard_map(
        on_device, mesh=mesh, in_specs=in_specs, out_specs=out_specs, check_vma=False
    )
```

```python
import jax
import jax.numpy as jnp
from jax import lax
from jax.sharding import PartitionSpec as P

EDGE = 8
CELLS = 512
BX_SEG = 3
LB_DEV = 128
BPD = 384


def shifted(value, axis, steps):
    count = lax.axis_size(axis)
    first, last = (max(0, -steps), min(count, count - steps))
    return lax.ppermute(value, axis, [(source, source + steps) for source in range(first, last)])


def padded(block, sides, width):
    for axis, dim in sides:
        count = lax.axis_size(axis)
        forward = [(i, i + 1) for i in range(count - 1)]
        backward = [(target, source) for source, target in forward]
        low = lax.ppermute(
            lax.slice_in_dim(block, block.shape[dim] - width, None, axis=dim), axis, forward
        )
        high = lax.ppermute(lax.slice_in_dim(block, 0, width, axis=dim), axis, backward)
        block = jnp.concatenate([low, block, high], axis=dim)
    return block


def combine_rows(row_set, before, after_rows, left_ok, right_ok):
    alpha = jnp.where(
        left_ok, -row_set[..., 0, :] / jnp.where(left_ok, before[..., 1, :], 1.0), 0.0
    )
    gamma = jnp.where(
        right_ok, -row_set[..., 2, :] / jnp.where(right_ok, after_rows[..., 1, :], 1.0), 0.0
    )
    new_lower = alpha * before[..., 0, :]
    new_upper = gamma * after_rows[..., 2, :]
    new_main = row_set[..., 1, :] + alpha * before[..., 2, :] + gamma * after_rows[..., 0, :]
    new_right = (
        row_set[..., 3:, :]
        + alpha[..., None, :] * before[..., 3:, :]
        + gamma[..., None, :] * after_rows[..., 3:, :]
    )
    return jnp.concatenate(
        [new_lower[..., None, :], new_main[..., None, :], new_upper[..., None, :], new_right],
        axis=-2,
    )


def neighbours(left_part, right_part, offset):
    from_left = shifted(left_part, "pencil", offset)
    from_right = shifted(right_part, "pencil", -offset)
    return (from_left, from_right)


def on_device(velocity, viscosity, density, slot_block):
    n_pencil = lax.axis_size("pencil")
    n_group = lax.axis_size("group")
    devices = n_pencil * n_group
    n_slots = slot_block.shape[0]
    capacity = n_slots // devices
    blocks_x = BX_SEG * n_pencil
    edge_sq = EDGE * EDGE
    seg_width = EDGE * BX_SEG
    lines_here = LB_DEV * edge_sq
    live_slot = slot_block >= 0
    safe_ids = jnp.where(live_slot, slot_block, 0)
    block_x = safe_ids % blocks_x
    block_line = safe_ids // blocks_x
    target = block_x // BX_SEG * n_group + block_line // LB_DEV
    one_hot = jnp.logical_and(
        target[:, None] == jnp.arange(devices, dtype=jnp.int32)[None, :], live_slot[:, None]
    ).astype(jnp.int32)
    target_rank = jnp.sum((jnp.cumsum(one_hot, axis=0) - 1) * one_hot, axis=1)
    position = jnp.where(live_slot, target * capacity + target_rank, devices * capacity)
    source_of = (
        jnp.full((devices * capacity,), n_slots, jnp.int32)
        .at[position]
        .set(jnp.arange(n_slots, dtype=jnp.int32), mode="drop")
    )
    lane_rows = CELLS // 128
    send_flow = jnp.take(velocity.reshape(n_slots, 3 * lane_rows, 128), source_of, axis=0, mode="clip")
    pair = jnp.stack([viscosity, density], axis=1).reshape(n_slots, 2 * lane_rows, 128)
    send_pair = jnp.take(pair, source_of, axis=0, mode="clip")
    labels = jnp.take(slot_block, source_of, axis=0, mode="fill", fill_value=-1)
    got_flow, got_pair, arrived_ids = (
        lax.all_to_all(
            send_flow.reshape(devices, capacity * 3 * lane_rows, 128),
            ("pencil", "group"),
            split_axis=0,
            concat_axis=0,
            tiled=True,
        ),
        lax.all_to_all(
            send_pair.reshape(devices, capacity * 2 * lane_rows, 128),
            ("pencil", "group"),
            split_axis=0,
            concat_axis=0,
            tiled=True,
        ),
        lax.all_to_all(
            labels.reshape(devices, capacity),
            ("pencil", "group"),
            split_axis=0,
            concat_axis=0,
            tiled=True,
        ),
    )
    n_arrived = devices * capacity
    got_flow = got_flow.reshape(n_arrived, 3, CELLS)
    got_pair = got_pair.reshape(n_arrived, 2, CELLS)
    got_visc = got_pair[:, 0]
    got_mass = got_pair[:, 1]
    arrived_ids = arrived_ids.reshape(n_arrived)
    pencil_at = lax.axis_index("pencil")
    group_at = lax.axis_index("group")
    arrive_live = arrived_ids >= 0
    arrive_safe = jnp.where(arrive_live, arrived_ids, 0)
    local_block = (arrive_safe // blocks_x - group_at * LB_DEV) * BX_SEG + (
        arrive_safe % blocks_x - pencil_at * BX_SEG
    )
    local_block = jnp.where(arrive_live, local_block, BPD).astype(jnp.int32)
    which_arrived = (
        jnp.full((BPD,), n_arrived, jnp.int32)
        .at[local_block]
        .set(jnp.arange(n_arrived, dtype=jnp.int32), mode="drop")
    )
    block_active = (which_arrived < n_arrived).astype(jnp.float32)
    tile_flow = jnp.take(got_flow, which_arrived, axis=0, mode="clip")
    tile_visc = jnp.take(got_visc, which_arrived, axis=0, mode="clip")
    tile_mass = jnp.take(got_mass, which_arrived, axis=0, mode="fill", fill_value=0.0)
    flow_grid = (
        tile_flow.reshape(LB_DEV, BX_SEG, 3, EDGE, edge_sq)
        .transpose(2, 1, 3, 0, 4)
        .reshape(3, seg_width, lines_here)
    )
    visc_grid = (
        tile_visc.reshape(LB_DEV, BX_SEG, EDGE, edge_sq)
        .transpose(1, 2, 0, 3)
        .reshape(seg_width, lines_here)
    )
    mass_grid = (
        tile_mass.reshape(LB_DEV, BX_SEG, EDGE, edge_sq)
        .transpose(1, 2, 0, 3)
        .reshape(seg_width, lines_here)
    )
    active = jnp.broadcast_to(
        block_active.reshape(LB_DEV, BX_SEG).T[:, None, :, None], (BX_SEG, EDGE, LB_DEV, edge_sq)
    ).reshape(seg_width, lines_here)
    rimmed = padded(jnp.stack([visc_grid, active], axis=0), (("pencil", 1),), 1)
    face_visc = 0.5 * (rimmed[0, :-1] + rimmed[0, 1:]) * rimmed[1, :-1] * rimmed[1, 1:]
    face_left = face_visc[:-1]
    face_right = face_visc[1:]
    lower_band = -face_left
    upper_band = -face_right
    main_band = mass_grid + face_left + face_right + (1.0 - active)
    right_side = mass_grid[None] * flow_grid
    prev_lower = -jnp.ones((lines_here,), jnp.float32)
    prev_upper = jnp.zeros((lines_here,), jnp.float32)
    prev_right = jnp.zeros((3, lines_here), jnp.float32)
    fwd_lower, fwd_upper, fwd_right = ([], [], [])
    for cell_x in range(1, seg_width):
        low_coef = lower_band[cell_x]
        pivot_inv = 1.0 / (main_band[cell_x] - low_coef * prev_upper)
        prev_lower = -low_coef * prev_lower * pivot_inv
        prev_upper = upper_band[cell_x] * pivot_inv
        prev_right = (right_side[:, cell_x] - low_coef[None, :] * prev_right) * pivot_inv[None, :]
        fwd_lower.append(prev_lower)
        fwd_upper.append(prev_upper)
        fwd_right.append(prev_right)
    next_lower = jnp.zeros((lines_here,), jnp.float32)
    next_upper = -jnp.ones((lines_here,), jnp.float32)
    next_right = jnp.zeros((3, lines_here), jnp.float32)
    back_lower = [None] * (seg_width - 2)
    back_upper = [None] * (seg_width - 2)
    back_right = [None] * (seg_width - 2)
    for index_k in range(seg_width - 3, -1, -1):
        row_upper = fwd_upper[index_k]
        next_right = fwd_right[index_k] - row_upper[None, :] * next_right
        next_lower = fwd_lower[index_k] - row_upper * next_lower
        next_upper = -row_upper * next_upper
        back_lower[index_k] = next_lower
        back_upper[index_k] = next_upper
        back_right[index_k] = next_right
    first_row = jnp.concatenate(
        [
            lower_band[0][None],
            (main_band[0] - upper_band[0] * back_lower[0])[None],
            (-upper_band[0] * back_upper[0])[None],
            right_side[:, 0] - upper_band[0][None, :] * back_right[0],
        ],
        axis=0,
    )
    last_row = jnp.concatenate(
        [
            fwd_lower[-1][None],
            jnp.ones((1, lines_here), jnp.float32),
            fwd_upper[-1][None],
            fwd_right[-1],
        ],
        axis=0,
    )
    reduced = jnp.stack([first_row, last_row])
    chunk = lines_here // n_pencil
    sent_rows = reduced.reshape(2, 6, n_pencil, chunk).transpose(2, 0, 1, 3)
    all_rows = lax.all_to_all(sent_rows, "pencil", 0, 0, tiled=True)
    all_rows = all_rows.reshape(2 * n_pencil, 6, chunk)
    scaled_upper = []
    scaled_right = []
    carry_upper = jnp.zeros((chunk,), jnp.float32)
    carry_right = jnp.zeros((3, chunk), jnp.float32)
    for row_at in range(2 * n_pencil):
        row_lower = all_rows[row_at, 0]
        row_inv = 1.0 / (all_rows[row_at, 1] - row_lower * carry_upper)
        carry_upper = all_rows[row_at, 2] * row_inv
        carry_right = (all_rows[row_at, 3:] - row_lower[None, :] * carry_right) * row_inv[None, :]
        scaled_upper.append(carry_upper)
        scaled_right.append(carry_right)
    ends = [None] * (2 * n_pencil)
    ends[-1] = scaled_right[-1]
    for row_at in range(2 * n_pencil - 2, -1, -1):
        ends[row_at] = scaled_right[row_at] - scaled_upper[row_at][None, :] * ends[row_at + 1]
    solved_ends = jnp.stack(ends).reshape(n_pencil, 2, 3, chunk)
    solved_ends = lax.all_to_all(solved_ends, "pencil", 0, 0, tiled=True)
    solution_ends = solved_ends.transpose(1, 2, 0, 3).reshape(2, 3, lines_here)
    end_first = solution_ends[0]
    end_last = solution_ends[1]
    columns = [end_first]
    for index_k in range(seg_width - 2):
        columns.append(
            back_right[index_k]
            - back_lower[index_k][None, :] * end_first
            - back_upper[index_k][None, :] * end_last
        )
    columns.append(end_last)
    return jnp.stack(columns, axis=1)


def solution(mesh):
    in_specs = (
        P(("pencil", "group"), None, None),
        P(("pencil", "group"), None),
        P(("pencil", "group"), None),
        P(("pencil", "group")),
    )
    out_specs = P(None, "pencil", "group")
    return jax.shard_map(
        on_device, mesh=mesh, in_specs=in_specs, out_specs=out_specs, check_vma=False
    )
```

```python
import jax
import jax.numpy as jnp
from jax import lax
from jax.sharding import PartitionSpec as P

EDGE = 8
CELLS = 512
BX_SEG = 3
LB_DEV = 128
BPD = 384


def shifted(value, axis, steps):
    count = lax.axis_size(axis)
    first, last = (max(0, -steps), min(count, count - steps))
    return lax.ppermute(value, axis, [(source, source + steps) for source in range(first, last)])


def padded(block, sides, width):
    for axis, dim in sides:
        count = lax.axis_size(axis)
        forward = [(i, i + 1) for i in range(count - 1)]
        backward = [(target, source) for source, target in forward]
        low = lax.ppermute(
            lax.slice_in_dim(block, block.shape[dim] - width, None, axis=dim), axis, forward
        )
        high = lax.ppermute(lax.slice_in_dim(block, 0, width, axis=dim), axis, backward)
        block = jnp.concatenate([low, block, high], axis=dim)
    return block


def combine_rows(row_set, before, after_rows, left_ok, right_ok):
    alpha = jnp.where(
        left_ok, -row_set[..., 0, :] / jnp.where(left_ok, before[..., 1, :], 1.0), 0.0
    )
    gamma = jnp.where(
        right_ok, -row_set[..., 2, :] / jnp.where(right_ok, after_rows[..., 1, :], 1.0), 0.0
    )
    new_lower = alpha * before[..., 0, :]
    new_upper = gamma * after_rows[..., 2, :]
    new_main = row_set[..., 1, :] + alpha * before[..., 2, :] + gamma * after_rows[..., 0, :]
    new_right = (
        row_set[..., 3:, :]
        + alpha[..., None, :] * before[..., 3:, :]
        + gamma[..., None, :] * after_rows[..., 3:, :]
    )
    return jnp.concatenate(
        [new_lower[..., None, :], new_main[..., None, :], new_upper[..., None, :], new_right],
        axis=-2,
    )


def neighbours(left_part, right_part, offset):
    from_left = shifted(left_part, "pencil", offset)
    from_right = shifted(right_part, "pencil", -offset)
    return (from_left, from_right)


def on_device(velocity, viscosity, density, slot_block):
    n_pencil = lax.axis_size("pencil")
    n_group = lax.axis_size("group")
    devices = n_pencil * n_group
    n_slots = slot_block.shape[0]
    capacity = n_slots // devices
    blocks_x = BX_SEG * n_pencil
    edge_sq = EDGE * EDGE
    seg_width = EDGE * BX_SEG
    lines_here = LB_DEV * edge_sq
    live_slot = slot_block >= 0
    safe_ids = jnp.where(live_slot, slot_block, 0)
    block_x = safe_ids % blocks_x
    block_line = safe_ids // blocks_x
    target = block_x // BX_SEG * n_group + block_line // LB_DEV
    one_hot = jnp.logical_and(
        target[:, None] == jnp.arange(devices, dtype=jnp.int32)[None, :], live_slot[:, None]
    ).astype(jnp.int32)
    target_rank = jnp.sum((jnp.cumsum(one_hot, axis=0) - 1) * one_hot, axis=1)
    position = jnp.where(live_slot, target * capacity + target_rank, devices * capacity)
    source_of = (
        jnp.full((devices * capacity,), n_slots, jnp.int32)
        .at[position]
        .set(jnp.arange(n_slots, dtype=jnp.int32), mode="drop")
    )
    lane_rows = CELLS // 128
    send_flow = jnp.take(velocity.reshape(n_slots, 3 * lane_rows, 128), source_of, axis=0, mode="clip")
    pair = jnp.stack([viscosity, density], axis=1).reshape(n_slots, 2 * lane_rows, 128)
    send_pair = jnp.take(pair, source_of, axis=0, mode="clip")
    labels = jnp.take(slot_block, source_of, axis=0, mode="fill", fill_value=-1)
    label_row = jnp.pad(
        labels.reshape(devices, 1, capacity).astype(jnp.float32), ((0, 0), (0, 0), (0, 128 - capacity))
    )
    send_pair = jnp.concatenate(
        [send_pair.reshape(devices, capacity * 2 * lane_rows, 128), label_row], axis=1
    )
    got_pair = lax.all_to_all(send_pair, ("pencil", "group"), 0, 0, tiled=True)
    got_pair, send_flow = lax.optimization_barrier((got_pair, send_flow))
    got_flow = lax.all_to_all(
        send_flow.reshape(devices, capacity * 3 * lane_rows, 128),
        ("pencil", "group"),
        split_axis=0,
        concat_axis=0,
        tiled=True,
    )
    n_arrived = devices * capacity
    arrived_ids = got_pair[:, capacity * 2 * lane_rows, :capacity].astype(jnp.int32).reshape(n_arrived)
    got_pair = got_pair[:, : capacity * 2 * lane_rows].reshape(n_arrived, 2, CELLS)
    got_flow = got_flow.reshape(n_arrived, 3, CELLS)
    got_visc = got_pair[:, 0]
    got_mass = got_pair[:, 1]
    pencil_at = lax.axis_index("pencil")
    group_at = lax.axis_index("group")
    arrive_live = arrived_ids >= 0
    arrive_safe = jnp.where(arrive_live, arrived_ids, 0)
    local_block = (arrive_safe // blocks_x - group_at * LB_DEV) * BX_SEG + (
        arrive_safe % blocks_x - pencil_at * BX_SEG
    )
    local_block = jnp.where(arrive_live, local_block, BPD).astype(jnp.int32)
    which_arrived = (
        jnp.full((BPD,), n_arrived, jnp.int32)
        .at[local_block]
        .set(jnp.arange(n_arrived, dtype=jnp.int32), mode="drop")
    )
    block_active = (which_arrived < n_arrived).astype(jnp.float32)
    tile_flow = jnp.take(got_flow, which_arrived, axis=0, mode="clip")
    tile_visc = jnp.take(got_visc, which_arrived, axis=0, mode="clip")
    tile_mass = jnp.take(got_mass, which_arrived, axis=0, mode="fill", fill_value=0.0)
    flow_grid = (
        tile_flow.reshape(LB_DEV, BX_SEG, 3, EDGE, edge_sq)
        .transpose(2, 1, 3, 0, 4)
        .reshape(3, seg_width, lines_here)
    )
    visc_grid = (
        tile_visc.reshape(LB_DEV, BX_SEG, EDGE, edge_sq)
        .transpose(1, 2, 0, 3)
        .reshape(seg_width, lines_here)
    )
    mass_grid = (
        tile_mass.reshape(LB_DEV, BX_SEG, EDGE, edge_sq)
        .transpose(1, 2, 0, 3)
        .reshape(seg_width, lines_here)
    )
    active = jnp.broadcast_to(
        block_active.reshape(LB_DEV, BX_SEG).T[:, None, :, None], (BX_SEG, EDGE, LB_DEV, edge_sq)
    ).reshape(seg_width, lines_here)
    rimmed = padded(jnp.stack([visc_grid, active], axis=0), (("pencil", 1),), 1)
    face_visc = 0.5 * (rimmed[0, :-1] + rimmed[0, 1:]) * rimmed[1, :-1] * rimmed[1, 1:]
    face_left = face_visc[:-1]
    face_right = face_visc[1:]
    lower_band = -face_left
    upper_band = -face_right
    main_band = mass_grid + face_left + face_right + (1.0 - active)
    right_side = mass_grid[None] * flow_grid
    prev_lower = -jnp.ones((lines_here,), jnp.float32)
    prev_upper = jnp.zeros((lines_here,), jnp.float32)
    prev_right = jnp.zeros((3, lines_here), jnp.float32)
    fwd_lower, fwd_upper, fwd_right = ([], [], [])
    for cell_x in range(1, seg_width):
        low_coef = lower_band[cell_x]
        pivot_inv = 1.0 / (main_band[cell_x] - low_coef * prev_upper)
        prev_lower = -low_coef * prev_lower * pivot_inv
        prev_upper = upper_band[cell_x] * pivot_inv
        prev_right = (right_side[:, cell_x] - low_coef[None, :] * prev_right) * pivot_inv[None, :]
        fwd_lower.append(prev_lower)
        fwd_upper.append(prev_upper)
        fwd_right.append(prev_right)
    next_lower = jnp.zeros((lines_here,), jnp.float32)
    next_upper = -jnp.ones((lines_here,), jnp.float32)
    next_right = jnp.zeros((3, lines_here), jnp.float32)
    back_lower = [None] * (seg_width - 2)
    back_upper = [None] * (seg_width - 2)
    back_right = [None] * (seg_width - 2)
    for index_k in range(seg_width - 3, -1, -1):
        row_upper = fwd_upper[index_k]
        next_right = fwd_right[index_k] - row_upper[None, :] * next_right
        next_lower = fwd_lower[index_k] - row_upper * next_lower
        next_upper = -row_upper * next_upper
        back_lower[index_k] = next_lower
        back_upper[index_k] = next_upper
        back_right[index_k] = next_right
    first_row = jnp.concatenate(
        [
            lower_band[0][None],
            (main_band[0] - upper_band[0] * back_lower[0])[None],
            (-upper_band[0] * back_upper[0])[None],
            right_side[:, 0] - upper_band[0][None, :] * back_right[0],
        ],
        axis=0,
    )
    last_row = jnp.concatenate(
        [
            fwd_lower[-1][None],
            jnp.ones((1, lines_here), jnp.float32),
            fwd_upper[-1][None],
            fwd_right[-1],
        ],
        axis=0,
    )
    reduced = jnp.stack([first_row, last_row])
    chunk = lines_here // n_pencil
    sent_rows = reduced.reshape(2, 6, n_pencil, chunk).transpose(2, 0, 1, 3)
    all_rows = lax.all_to_all(sent_rows, "pencil", 0, 0, tiled=True)
    all_rows = all_rows.reshape(2 * n_pencil, 6, chunk)
    scaled_upper = []
    scaled_right = []
    carry_upper = jnp.zeros((chunk,), jnp.float32)
    carry_right = jnp.zeros((3, chunk), jnp.float32)
    for row_at in range(2 * n_pencil):
        row_lower = all_rows[row_at, 0]
        row_inv = 1.0 / (all_rows[row_at, 1] - row_lower * carry_upper)
        carry_upper = all_rows[row_at, 2] * row_inv
        carry_right = (all_rows[row_at, 3:] - row_lower[None, :] * carry_right) * row_inv[None, :]
        scaled_upper.append(carry_upper)
        scaled_right.append(carry_right)
    ends = [None] * (2 * n_pencil)
    ends[-1] = scaled_right[-1]
    for row_at in range(2 * n_pencil - 2, -1, -1):
        ends[row_at] = scaled_right[row_at] - scaled_upper[row_at][None, :] * ends[row_at + 1]
    solved_ends = jnp.stack(ends).reshape(n_pencil, 2, 3, chunk)
    solved_ends = lax.all_to_all(solved_ends, "pencil", 0, 0, tiled=True)
    solution_ends = solved_ends.transpose(1, 2, 0, 3).reshape(2, 3, lines_here)
    end_first = solution_ends[0]
    end_last = solution_ends[1]
    columns = [end_first]
    for index_k in range(seg_width - 2):
        columns.append(
            back_right[index_k]
            - back_lower[index_k][None, :] * end_first
            - back_upper[index_k][None, :] * end_last
        )
    columns.append(end_last)
    return jnp.stack(columns, axis=1)


def solution(mesh):
    in_specs = (
        P(("pencil", "group"), None, None),
        P(("pencil", "group"), None),
        P(("pencil", "group"), None),
        P(("pencil", "group")),
    )
    out_specs = P(None, "pencil", "group")
    return jax.shard_map(
        on_device, mesh=mesh, in_specs=in_specs, out_specs=out_specs, check_vma=False
    )
```

```python
import jax
import jax.numpy as jnp
from jax import lax
from jax.sharding import PartitionSpec as P

EDGE = 8
CELLS = 512
BX_SEG = 3
LB_DEV = 128
BPD = 384


def shifted(value, axis, steps):
    count = lax.axis_size(axis)
    first, last = (max(0, -steps), min(count, count - steps))
    return lax.ppermute(value, axis, [(source, source + steps) for source in range(first, last)])


def padded(block, sides, width):
    for axis, dim in sides:
        count = lax.axis_size(axis)
        forward = [(i, i + 1) for i in range(count - 1)]
        backward = [(target, source) for source, target in forward]
        low = lax.ppermute(
            lax.slice_in_dim(block, block.shape[dim] - width, None, axis=dim), axis, forward
        )
        high = lax.ppermute(lax.slice_in_dim(block, 0, width, axis=dim), axis, backward)
        block = jnp.concatenate([low, block, high], axis=dim)
    return block


def combine_rows(row_set, before, after_rows, left_ok, right_ok):
    alpha = jnp.where(
        left_ok, -row_set[..., 0, :] / jnp.where(left_ok, before[..., 1, :], 1.0), 0.0
    )
    gamma = jnp.where(
        right_ok, -row_set[..., 2, :] / jnp.where(right_ok, after_rows[..., 1, :], 1.0), 0.0
    )
    new_lower = alpha * before[..., 0, :]
    new_upper = gamma * after_rows[..., 2, :]
    new_main = row_set[..., 1, :] + alpha * before[..., 2, :] + gamma * after_rows[..., 0, :]
    new_right = (
        row_set[..., 3:, :]
        + alpha[..., None, :] * before[..., 3:, :]
        + gamma[..., None, :] * after_rows[..., 3:, :]
    )
    return jnp.concatenate(
        [new_lower[..., None, :], new_main[..., None, :], new_upper[..., None, :], new_right],
        axis=-2,
    )


def neighbours(left_part, right_part, offset):
    from_left = shifted(left_part, "pencil", offset)
    from_right = shifted(right_part, "pencil", -offset)
    return (from_left, from_right)


def on_device(velocity, viscosity, density, slot_block):
    n_pencil = lax.axis_size("pencil")
    n_group = lax.axis_size("group")
    devices = n_pencil * n_group
    n_slots = slot_block.shape[0]
    capacity = n_slots // devices
    blocks_x = BX_SEG * n_pencil
    edge_sq = EDGE * EDGE
    seg_width = EDGE * BX_SEG
    lines_here = LB_DEV * edge_sq
    live_slot = slot_block >= 0
    safe_ids = jnp.where(live_slot, slot_block, 0)
    block_x = safe_ids % blocks_x
    block_line = safe_ids // blocks_x
    target = block_x // BX_SEG * n_group + block_line // LB_DEV
    one_hot = jnp.logical_and(
        target[:, None] == jnp.arange(devices, dtype=jnp.int32)[None, :], live_slot[:, None]
    ).astype(jnp.int32)
    target_rank = jnp.sum((jnp.cumsum(one_hot, axis=0) - 1) * one_hot, axis=1)
    position = jnp.where(live_slot, target * capacity + target_rank, devices * capacity)
    source_of = (
        jnp.full((devices * capacity,), n_slots, jnp.int32)
        .at[position]
        .set(jnp.arange(n_slots, dtype=jnp.int32), mode="drop")
    )
    lane_rows = CELLS // 128
    send_flow = jnp.take(velocity.reshape(n_slots, 3 * lane_rows, 128), source_of, axis=0, mode="clip")
    pair = jnp.stack([viscosity, density], axis=1).reshape(n_slots, 2 * lane_rows, 128)
    send_pair = jnp.take(pair, source_of, axis=0, mode="clip")
    labels = jnp.take(slot_block, source_of, axis=0, mode="fill", fill_value=-1)
    label_row = jnp.pad(
        labels.reshape(devices, 1, capacity).astype(jnp.float32), ((0, 0), (0, 0), (0, 128 - capacity))
    )
    send_pair = jnp.concatenate(
        [send_pair.reshape(devices, capacity * 2 * lane_rows, 128), label_row], axis=1
    )
    got_pair = lax.all_to_all(send_pair, ("pencil", "group"), 0, 0, tiled=True)
    got_pair, send_flow = lax.optimization_barrier((got_pair, send_flow))
    got_flow = lax.all_to_all(
        send_flow.reshape(devices, capacity * 3 * lane_rows, 128),
        ("pencil", "group"),
        split_axis=0,
        concat_axis=0,
        tiled=True,
    )
    n_arrived = devices * capacity
    arrived_ids = got_pair[:, capacity * 2 * lane_rows, :capacity].astype(jnp.int32).reshape(n_arrived)
    got_pair = got_pair[:, : capacity * 2 * lane_rows].reshape(n_arrived, 2, CELLS)
    got_flow = got_flow.reshape(n_arrived, 3, CELLS)
    got_visc = got_pair[:, 0]
    got_mass = got_pair[:, 1]
    pencil_at = lax.axis_index("pencil")
    group_at = lax.axis_index("group")
    arrive_live = arrived_ids >= 0
    arrive_safe = jnp.where(arrive_live, arrived_ids, 0)
    local_block = (arrive_safe // blocks_x - group_at * LB_DEV) * BX_SEG + (
        arrive_safe % blocks_x - pencil_at * BX_SEG
    )
    local_block = jnp.where(arrive_live, local_block, BPD).astype(jnp.int32)
    which_arrived = (
        jnp.full((BPD,), n_arrived, jnp.int32)
        .at[local_block]
        .set(jnp.arange(n_arrived, dtype=jnp.int32), mode="drop")
    )
    block_active = (which_arrived < n_arrived).astype(jnp.float32)
    tile_flow = jnp.take(got_flow, which_arrived, axis=0, mode="clip")
    tile_visc = jnp.take(got_visc, which_arrived, axis=0, mode="clip")
    tile_mass = jnp.take(got_mass, which_arrived, axis=0, mode="fill", fill_value=0.0)
    flow_grid = (
        tile_flow.reshape(LB_DEV, BX_SEG, 3, EDGE, edge_sq)
        .transpose(2, 1, 3, 0, 4)
        .reshape(3, seg_width, lines_here)
    )
    visc_grid = (
        tile_visc.reshape(LB_DEV, BX_SEG, EDGE, edge_sq)
        .transpose(1, 2, 0, 3)
        .reshape(seg_width, lines_here)
    )
    mass_grid = (
        tile_mass.reshape(LB_DEV, BX_SEG, EDGE, edge_sq)
        .transpose(1, 2, 0, 3)
        .reshape(seg_width, lines_here)
    )
    active = jnp.broadcast_to(
        block_active.reshape(LB_DEV, BX_SEG).T[:, None, :, None], (BX_SEG, EDGE, LB_DEV, edge_sq)
    ).reshape(seg_width, lines_here)
    rimmed = padded(jnp.stack([visc_grid, active], axis=0), (("pencil", 1),), 1)
    face_visc = 0.5 * (rimmed[0, :-1] + rimmed[0, 1:]) * rimmed[1, :-1] * rimmed[1, 1:]
    face_left = face_visc[:-1]
    face_right = face_visc[1:]
    lower_band = -face_left
    upper_band = -face_right
    main_band = mass_grid + face_left + face_right + (1.0 - active)
    right_side = mass_grid[None] * flow_grid
    prev_lower = -jnp.ones((lines_here,), jnp.float32)
    prev_upper = jnp.zeros((lines_here,), jnp.float32)
    prev_right = jnp.zeros((3, lines_here), jnp.float32)
    fwd_lower, fwd_upper, fwd_right = ([], [], [])
    for cell_x in range(1, seg_width):
        low_coef = lower_band[cell_x]
        pivot_inv = 1.0 / (main_band[cell_x] - low_coef * prev_upper)
        prev_lower = -low_coef * prev_lower * pivot_inv
        prev_upper = upper_band[cell_x] * pivot_inv
        prev_right = (right_side[:, cell_x] - low_coef[None, :] * prev_right) * pivot_inv[None, :]
        fwd_lower.append(prev_lower)
        fwd_upper.append(prev_upper)
        fwd_right.append(prev_right)
    next_lower = jnp.zeros((lines_here,), jnp.float32)
    next_upper = -jnp.ones((lines_here,), jnp.float32)
    next_right = jnp.zeros((3, lines_here), jnp.float32)
    back_lower = [None] * (seg_width - 2)
    back_upper = [None] * (seg_width - 2)
    back_right = [None] * (seg_width - 2)
    for index_k in range(seg_width - 3, -1, -1):
        row_upper = fwd_upper[index_k]
        next_right = fwd_right[index_k] - row_upper[None, :] * next_right
        next_lower = fwd_lower[index_k] - row_upper * next_lower
        next_upper = -row_upper * next_upper
        back_lower[index_k] = next_lower
        back_upper[index_k] = next_upper
        back_right[index_k] = next_right
    first_row = jnp.concatenate(
        [
            lower_band[0][None],
            (main_band[0] - upper_band[0] * back_lower[0])[None],
            (-upper_band[0] * back_upper[0])[None],
            right_side[:, 0] - upper_band[0][None, :] * back_right[0],
        ],
        axis=0,
    )
    last_row = jnp.concatenate(
        [
            fwd_lower[-1][None],
            jnp.ones((1, lines_here), jnp.float32),
            fwd_upper[-1][None],
            fwd_right[-1],
        ],
        axis=0,
    )
    reduced = jnp.stack([first_row, last_row])
    chunk = lines_here // n_pencil
    sent_rows = reduced.reshape(2, 6, n_pencil, chunk).transpose(2, 0, 1, 3)
    sent_rows = sent_rows.reshape(n_pencil, 12 * chunk // 128, 128)
    all_rows = lax.all_to_all(sent_rows, "pencil", 0, 0, tiled=True)
    all_rows = all_rows.reshape(2 * n_pencil, 6, chunk)
    scaled_upper = []
    scaled_right = []
    carry_upper = jnp.zeros((chunk,), jnp.float32)
    carry_right = jnp.zeros((3, chunk), jnp.float32)
    for row_at in range(2 * n_pencil):
        row_lower = all_rows[row_at, 0]
        row_inv = 1.0 / (all_rows[row_at, 1] - row_lower * carry_upper)
        carry_upper = all_rows[row_at, 2] * row_inv
        carry_right = (all_rows[row_at, 3:] - row_lower[None, :] * carry_right) * row_inv[None, :]
        scaled_upper.append(carry_upper)
        scaled_right.append(carry_right)
    ends = [None] * (2 * n_pencil)
    ends[-1] = scaled_right[-1]
    for row_at in range(2 * n_pencil - 2, -1, -1):
        ends[row_at] = scaled_right[row_at] - scaled_upper[row_at][None, :] * ends[row_at + 1]
    solved_ends = jnp.stack(ends).reshape(n_pencil, 6 * chunk // 128, 128)
    solved_ends = lax.all_to_all(solved_ends, "pencil", 0, 0, tiled=True)
    solved_ends = solved_ends.reshape(n_pencil, 2, 3, chunk)
    solution_ends = solved_ends.transpose(1, 2, 0, 3).reshape(2, 3, lines_here)
    end_first = solution_ends[0]
    end_last = solution_ends[1]
    columns = [end_first]
    for index_k in range(seg_width - 2):
        columns.append(
            back_right[index_k]
            - back_lower[index_k][None, :] * end_first
            - back_upper[index_k][None, :] * end_last
        )
    columns.append(end_last)
    return jnp.stack(columns, axis=1)


def solution(mesh):
    in_specs = (
        P(("pencil", "group"), None, None),
        P(("pencil", "group"), None),
        P(("pencil", "group"), None),
        P(("pencil", "group")),
    )
    out_specs = P(None, "pencil", "group")
    return jax.shard_map(
        on_device, mesh=mesh, in_specs=in_specs, out_specs=out_specs, check_vma=False
    )
```

```python
import jax
import jax.numpy as jnp
from jax import lax
from jax.sharding import PartitionSpec as P

EDGE = 8
CELLS = 512
BX_SEG = 3
LB_DEV = 128
BPD = 384


def shifted(value, axis, steps):
    count = lax.axis_size(axis)
    first, last = (max(0, -steps), min(count, count - steps))
    return lax.ppermute(value, axis, [(source, source + steps) for source in range(first, last)])


def padded(block, sides, width):
    for axis, dim in sides:
        count = lax.axis_size(axis)
        forward = [(i, i + 1) for i in range(count - 1)]
        backward = [(target, source) for source, target in forward]
        low = lax.ppermute(
            lax.slice_in_dim(block, block.shape[dim] - width, None, axis=dim), axis, forward
        )
        high = lax.ppermute(lax.slice_in_dim(block, 0, width, axis=dim), axis, backward)
        block = jnp.concatenate([low, block, high], axis=dim)
    return block


def combine_rows(row_set, before, after_rows, left_ok, right_ok):
    alpha = jnp.where(
        left_ok, -row_set[..., 0, :] / jnp.where(left_ok, before[..., 1, :], 1.0), 0.0
    )
    gamma = jnp.where(
        right_ok, -row_set[..., 2, :] / jnp.where(right_ok, after_rows[..., 1, :], 1.0), 0.0
    )
    new_lower = alpha * before[..., 0, :]
    new_upper = gamma * after_rows[..., 2, :]
    new_main = row_set[..., 1, :] + alpha * before[..., 2, :] + gamma * after_rows[..., 0, :]
    new_right = (
        row_set[..., 3:, :]
        + alpha[..., None, :] * before[..., 3:, :]
        + gamma[..., None, :] * after_rows[..., 3:, :]
    )
    return jnp.concatenate(
        [new_lower[..., None, :], new_main[..., None, :], new_upper[..., None, :], new_right],
        axis=-2,
    )


def neighbours(left_part, right_part, offset):
    from_left = shifted(left_part, "pencil", offset)
    from_right = shifted(right_part, "pencil", -offset)
    return (from_left, from_right)


def on_device(velocity, viscosity, density, slot_block):
    n_pencil = lax.axis_size("pencil")
    n_group = lax.axis_size("group")
    devices = n_pencil * n_group
    n_slots = slot_block.shape[0]
    capacity = n_slots // devices
    blocks_x = BX_SEG * n_pencil
    edge_sq = EDGE * EDGE
    seg_width = EDGE * BX_SEG
    lines_here = LB_DEV * edge_sq
    live_slot = slot_block >= 0
    safe_ids = jnp.where(live_slot, slot_block, 0)
    block_x = safe_ids % blocks_x
    block_line = safe_ids // blocks_x
    target = block_x // BX_SEG * n_group + block_line // LB_DEV
    one_hot = jnp.logical_and(
        target[:, None] == jnp.arange(devices, dtype=jnp.int32)[None, :], live_slot[:, None]
    ).astype(jnp.int32)
    target_rank = jnp.sum((jnp.cumsum(one_hot, axis=0) - 1) * one_hot, axis=1)
    position = jnp.where(live_slot, target * capacity + target_rank, devices * capacity)
    source_of = (
        jnp.full((devices * capacity,), n_slots, jnp.int32)
        .at[position]
        .set(jnp.arange(n_slots, dtype=jnp.int32), mode="drop")
    )
    lane_rows = CELLS // 128
    send_flow = jnp.take(velocity.reshape(n_slots, 3 * lane_rows, 128), source_of, axis=0, mode="clip")
    pair = jnp.stack([viscosity, density], axis=1).reshape(n_slots, 2 * lane_rows, 128)
    send_pair = jnp.take(pair, source_of, axis=0, mode="clip")
    labels = jnp.take(slot_block, source_of, axis=0, mode="fill", fill_value=-1)
    label_row = jnp.pad(
        labels.reshape(devices, 1, capacity).astype(jnp.float32), ((0, 0), (0, 0), (0, 128 - capacity))
    )
    pair_rows = capacity * 2 * lane_rows
    flow_rows = capacity * 3 * lane_rows
    send_all = jnp.concatenate(
        [
            send_pair.reshape(devices, pair_rows, 128),
            send_flow.reshape(devices, flow_rows, 128),
            label_row,
        ],
        axis=1,
    )
    got_all = lax.all_to_all(send_all, ("pencil", "group"), 0, 0, tiled=True)
    n_arrived = devices * capacity
    arrived_ids = got_all[:, pair_rows + flow_rows, :capacity].astype(jnp.int32).reshape(n_arrived)
    got_pair = got_all[:, :pair_rows].reshape(n_arrived, 2, CELLS)
    got_flow = got_all[:, pair_rows : pair_rows + flow_rows].reshape(n_arrived, 3, CELLS)
    got_visc = got_pair[:, 0]
    got_mass = got_pair[:, 1]
    pencil_at = lax.axis_index("pencil")
    group_at = lax.axis_index("group")
    arrive_live = arrived_ids >= 0
    arrive_safe = jnp.where(arrive_live, arrived_ids, 0)
    local_block = (arrive_safe // blocks_x - group_at * LB_DEV) * BX_SEG + (
        arrive_safe % blocks_x - pencil_at * BX_SEG
    )
    local_block = jnp.where(arrive_live, local_block, BPD).astype(jnp.int32)
    which_arrived = (
        jnp.full((BPD,), n_arrived, jnp.int32)
        .at[local_block]
        .set(jnp.arange(n_arrived, dtype=jnp.int32), mode="drop")
    )
    block_active = (which_arrived < n_arrived).astype(jnp.float32)
    tile_flow = jnp.take(got_flow, which_arrived, axis=0, mode="clip")
    tile_visc = jnp.take(got_visc, which_arrived, axis=0, mode="clip")
    tile_mass = jnp.take(got_mass, which_arrived, axis=0, mode="fill", fill_value=0.0)
    flow_grid = (
        tile_flow.reshape(LB_DEV, BX_SEG, 3, EDGE, edge_sq)
        .transpose(2, 1, 3, 0, 4)
        .reshape(3, seg_width, lines_here)
    )
    visc_grid = (
        tile_visc.reshape(LB_DEV, BX_SEG, EDGE, edge_sq)
        .transpose(1, 2, 0, 3)
        .reshape(seg_width, lines_here)
    )
    mass_grid = (
        tile_mass.reshape(LB_DEV, BX_SEG, EDGE, edge_sq)
        .transpose(1, 2, 0, 3)
        .reshape(seg_width, lines_here)
    )
    active = jnp.broadcast_to(
        block_active.reshape(LB_DEV, BX_SEG).T[:, None, :, None], (BX_SEG, EDGE, LB_DEV, edge_sq)
    ).reshape(seg_width, lines_here)
    rimmed = padded(jnp.stack([visc_grid, active], axis=0), (("pencil", 1),), 1)
    face_visc = 0.5 * (rimmed[0, :-1] + rimmed[0, 1:]) * rimmed[1, :-1] * rimmed[1, 1:]
    face_left = face_visc[:-1]
    face_right = face_visc[1:]
    lower_band = -face_left
    upper_band = -face_right
    main_band = mass_grid + face_left + face_right + (1.0 - active)
    right_side = mass_grid[None] * flow_grid
    prev_lower = -jnp.ones((lines_here,), jnp.float32)
    prev_upper = jnp.zeros((lines_here,), jnp.float32)
    prev_right = jnp.zeros((3, lines_here), jnp.float32)
    fwd_lower, fwd_upper, fwd_right = ([], [], [])
    for cell_x in range(1, seg_width):
        low_coef = lower_band[cell_x]
        pivot_inv = 1.0 / (main_band[cell_x] - low_coef * prev_upper)
        prev_lower = -low_coef * prev_lower * pivot_inv
        prev_upper = upper_band[cell_x] * pivot_inv
        prev_right = (right_side[:, cell_x] - low_coef[None, :] * prev_right) * pivot_inv[None, :]
        fwd_lower.append(prev_lower)
        fwd_upper.append(prev_upper)
        fwd_right.append(prev_right)
    next_lower = jnp.zeros((lines_here,), jnp.float32)
    next_upper = -jnp.ones((lines_here,), jnp.float32)
    next_right = jnp.zeros((3, lines_here), jnp.float32)
    back_lower = [None] * (seg_width - 2)
    back_upper = [None] * (seg_width - 2)
    back_right = [None] * (seg_width - 2)
    for index_k in range(seg_width - 3, -1, -1):
        row_upper = fwd_upper[index_k]
        next_right = fwd_right[index_k] - row_upper[None, :] * next_right
        next_lower = fwd_lower[index_k] - row_upper * next_lower
        next_upper = -row_upper * next_upper
        back_lower[index_k] = next_lower
        back_upper[index_k] = next_upper
        back_right[index_k] = next_right
    first_row = jnp.concatenate(
        [
            lower_band[0][None],
            (main_band[0] - upper_band[0] * back_lower[0])[None],
            (-upper_band[0] * back_upper[0])[None],
            right_side[:, 0] - upper_band[0][None, :] * back_right[0],
        ],
        axis=0,
    )
    last_row = jnp.concatenate(
        [
            fwd_lower[-1][None],
            jnp.ones((1, lines_here), jnp.float32),
            fwd_upper[-1][None],
            fwd_right[-1],
        ],
        axis=0,
    )
    reduced = jnp.stack([first_row, last_row])
    chunk = lines_here // n_pencil
    sent_rows = reduced.reshape(2, 6, n_pencil, chunk).transpose(2, 0, 1, 3)
    all_rows = lax.all_to_all(sent_rows, "pencil", 0, 0, tiled=True)
    all_rows = all_rows.reshape(2 * n_pencil, 6, chunk)
    scaled_upper = []
    scaled_right = []
    carry_upper = jnp.zeros((chunk,), jnp.float32)
    carry_right = jnp.zeros((3, chunk), jnp.float32)
    for row_at in range(2 * n_pencil):
        row_lower = all_rows[row_at, 0]
        row_inv = 1.0 / (all_rows[row_at, 1] - row_lower * carry_upper)
        carry_upper = all_rows[row_at, 2] * row_inv
        carry_right = (all_rows[row_at, 3:] - row_lower[None, :] * carry_right) * row_inv[None, :]
        scaled_upper.append(carry_upper)
        scaled_right.append(carry_right)
    ends = [None] * (2 * n_pencil)
    ends[-1] = scaled_right[-1]
    for row_at in range(2 * n_pencil - 2, -1, -1):
        ends[row_at] = scaled_right[row_at] - scaled_upper[row_at][None, :] * ends[row_at + 1]
    solved_ends = jnp.stack(ends).reshape(n_pencil, 2, 3, chunk)
    solved_ends = lax.all_to_all(solved_ends, "pencil", 0, 0, tiled=True)
    solution_ends = solved_ends.transpose(1, 2, 0, 3).reshape(2, 3, lines_here)
    end_first = solution_ends[0]
    end_last = solution_ends[1]
    columns = [end_first]
    for index_k in range(seg_width - 2):
        columns.append(
            back_right[index_k]
            - back_lower[index_k][None, :] * end_first
            - back_upper[index_k][None, :] * end_last
        )
    columns.append(end_last)
    return jnp.stack(columns, axis=1)


def solution(mesh):
    in_specs = (
        P(("pencil", "group"), None, None),
        P(("pencil", "group"), None),
        P(("pencil", "group"), None),
        P(("pencil", "group")),
    )
    out_specs = P(None, "pencil", "group")
    return jax.shard_map(
        on_device, mesh=mesh, in_specs=in_specs, out_specs=out_specs, check_vma=False
    )
```

```python
import jax
import jax.numpy as jnp
from jax import lax
from jax.sharding import PartitionSpec as P

EDGE = 8
CELLS = 512
BX_SEG = 3
LB_DEV = 128
BPD = 384


def shifted(value, axis, steps):
    count = lax.axis_size(axis)
    first, last = (max(0, -steps), min(count, count - steps))
    return lax.ppermute(value, axis, [(source, source + steps) for source in range(first, last)])


def padded(block, sides, width):
    for axis, dim in sides:
        count = lax.axis_size(axis)
        forward = [(i, i + 1) for i in range(count - 1)]
        backward = [(target, source) for source, target in forward]
        low = lax.ppermute(
            lax.slice_in_dim(block, block.shape[dim] - width, None, axis=dim), axis, forward
        )
        high = lax.ppermute(lax.slice_in_dim(block, 0, width, axis=dim), axis, backward)
        block = jnp.concatenate([low, block, high], axis=dim)
    return block


def combine_rows(row_set, before, after_rows, left_ok, right_ok):
    alpha = jnp.where(
        left_ok, -row_set[..., 0, :] / jnp.where(left_ok, before[..., 1, :], 1.0), 0.0
    )
    gamma = jnp.where(
        right_ok, -row_set[..., 2, :] / jnp.where(right_ok, after_rows[..., 1, :], 1.0), 0.0
    )
    new_lower = alpha * before[..., 0, :]
    new_upper = gamma * after_rows[..., 2, :]
    new_main = row_set[..., 1, :] + alpha * before[..., 2, :] + gamma * after_rows[..., 0, :]
    new_right = (
        row_set[..., 3:, :]
        + alpha[..., None, :] * before[..., 3:, :]
        + gamma[..., None, :] * after_rows[..., 3:, :]
    )
    return jnp.concatenate(
        [new_lower[..., None, :], new_main[..., None, :], new_upper[..., None, :], new_right],
        axis=-2,
    )


def neighbours(left_part, right_part, offset):
    from_left = shifted(left_part, "pencil", offset)
    from_right = shifted(right_part, "pencil", -offset)
    return (from_left, from_right)


def on_device(velocity, viscosity, density, slot_block):
    n_pencil = lax.axis_size("pencil")
    n_group = lax.axis_size("group")
    devices = n_pencil * n_group
    n_slots = slot_block.shape[0]
    capacity = n_slots // devices
    blocks_x = BX_SEG * n_pencil
    edge_sq = EDGE * EDGE
    seg_width = EDGE * BX_SEG
    lines_here = LB_DEV * edge_sq
    live_slot = slot_block >= 0
    safe_ids = jnp.where(live_slot, slot_block, 0)
    block_x = safe_ids % blocks_x
    block_line = safe_ids // blocks_x
    target = block_x // BX_SEG * n_group + block_line // LB_DEV
    one_hot = jnp.logical_and(
        target[:, None] == jnp.arange(devices, dtype=jnp.int32)[None, :], live_slot[:, None]
    ).astype(jnp.int32)
    target_rank = jnp.sum((jnp.cumsum(one_hot, axis=0) - 1) * one_hot, axis=1)
    position = jnp.where(live_slot, target * capacity + target_rank, devices * capacity)
    source_of = (
        jnp.full((devices * capacity,), n_slots, jnp.int32)
        .at[position]
        .set(jnp.arange(n_slots, dtype=jnp.int32), mode="drop")
    )
    lane_rows = CELLS // 128
    send_flow = jnp.take(velocity.reshape(n_slots, 3 * lane_rows, 128), source_of, axis=0, mode="clip")
    pair = jnp.stack([viscosity, density], axis=1).reshape(n_slots, 2 * lane_rows, 128)
    send_pair = jnp.take(pair, source_of, axis=0, mode="clip")
    labels = jnp.take(slot_block, source_of, axis=0, mode="fill", fill_value=-1)
    label_row = jnp.pad(
        labels.reshape(devices, 1, capacity).astype(jnp.float32), ((0, 0), (0, 0), (0, 128 - capacity))
    )
    flow_rows = capacity * 3 * lane_rows
    send_flow = jnp.concatenate(
        [send_flow.reshape(devices, flow_rows, 128), label_row], axis=1
    )
    got_flow = lax.all_to_all(send_flow, ("pencil", "group"), 0, 0, tiled=True)
    got_flow, send_pair = lax.optimization_barrier((got_flow, send_pair))
    got_pair = lax.all_to_all(
        send_pair.reshape(devices, capacity * 2 * lane_rows, 128),
        ("pencil", "group"),
        split_axis=0,
        concat_axis=0,
        tiled=True,
    )
    n_arrived = devices * capacity
    arrived_ids = got_flow[:, flow_rows, :capacity].astype(jnp.int32).reshape(n_arrived)
    got_flow = got_flow[:, :flow_rows].reshape(n_arrived, 3, CELLS)
    got_pair = got_pair.reshape(n_arrived, 2, CELLS)
    got_visc = got_pair[:, 0]
    got_mass = got_pair[:, 1]
    pencil_at = lax.axis_index("pencil")
    group_at = lax.axis_index("group")
    arrive_live = arrived_ids >= 0
    arrive_safe = jnp.where(arrive_live, arrived_ids, 0)
    local_block = (arrive_safe // blocks_x - group_at * LB_DEV) * BX_SEG + (
        arrive_safe % blocks_x - pencil_at * BX_SEG
    )
    local_block = jnp.where(arrive_live, local_block, BPD).astype(jnp.int32)
    which_arrived = (
        jnp.full((BPD,), n_arrived, jnp.int32)
        .at[local_block]
        .set(jnp.arange(n_arrived, dtype=jnp.int32), mode="drop")
    )
    block_active = (which_arrived < n_arrived).astype(jnp.float32)
    tile_flow = jnp.take(got_flow, which_arrived, axis=0, mode="clip")
    tile_visc = jnp.take(got_visc, which_arrived, axis=0, mode="clip")
    tile_mass = jnp.take(got_mass, which_arrived, axis=0, mode="fill", fill_value=0.0)
    flow_grid = (
        tile_flow.reshape(LB_DEV, BX_SEG, 3, EDGE, edge_sq)
        .transpose(2, 1, 3, 0, 4)
        .reshape(3, seg_width, lines_here)
    )
    visc_grid = (
        tile_visc.reshape(LB_DEV, BX_SEG, EDGE, edge_sq)
        .transpose(1, 2, 0, 3)
        .reshape(seg_width, lines_here)
    )
    mass_grid = (
        tile_mass.reshape(LB_DEV, BX_SEG, EDGE, edge_sq)
        .transpose(1, 2, 0, 3)
        .reshape(seg_width, lines_here)
    )
    active = jnp.broadcast_to(
        block_active.reshape(LB_DEV, BX_SEG).T[:, None, :, None], (BX_SEG, EDGE, LB_DEV, edge_sq)
    ).reshape(seg_width, lines_here)
    rimmed = padded(jnp.stack([visc_grid, active], axis=0), (("pencil", 1),), 1)
    face_visc = 0.5 * (rimmed[0, :-1] + rimmed[0, 1:]) * rimmed[1, :-1] * rimmed[1, 1:]
    face_left = face_visc[:-1]
    face_right = face_visc[1:]
    lower_band = -face_left
    upper_band = -face_right
    main_band = mass_grid + face_left + face_right + (1.0 - active)
    right_side = mass_grid[None] * flow_grid
    prev_lower = -jnp.ones((lines_here,), jnp.float32)
    prev_upper = jnp.zeros((lines_here,), jnp.float32)
    prev_right = jnp.zeros((3, lines_here), jnp.float32)
    fwd_lower, fwd_upper, fwd_right = ([], [], [])
    for cell_x in range(1, seg_width):
        low_coef = lower_band[cell_x]
        pivot_inv = 1.0 / (main_band[cell_x] - low_coef * prev_upper)
        prev_lower = -low_coef * prev_lower * pivot_inv
        prev_upper = upper_band[cell_x] * pivot_inv
        prev_right = (right_side[:, cell_x] - low_coef[None, :] * prev_right) * pivot_inv[None, :]
        fwd_lower.append(prev_lower)
        fwd_upper.append(prev_upper)
        fwd_right.append(prev_right)
    next_lower = jnp.zeros((lines_here,), jnp.float32)
    next_upper = -jnp.ones((lines_here,), jnp.float32)
    next_right = jnp.zeros((3, lines_here), jnp.float32)
    back_lower = [None] * (seg_width - 2)
    back_upper = [None] * (seg_width - 2)
    back_right = [None] * (seg_width - 2)
    for index_k in range(seg_width - 3, -1, -1):
        row_upper = fwd_upper[index_k]
        next_right = fwd_right[index_k] - row_upper[None, :] * next_right
        next_lower = fwd_lower[index_k] - row_upper * next_lower
        next_upper = -row_upper * next_upper
        back_lower[index_k] = next_lower
        back_upper[index_k] = next_upper
        back_right[index_k] = next_right
    first_row = jnp.concatenate(
        [
            lower_band[0][None],
            (main_band[0] - upper_band[0] * back_lower[0])[None],
            (-upper_band[0] * back_upper[0])[None],
            right_side[:, 0] - upper_band[0][None, :] * back_right[0],
        ],
        axis=0,
    )
    last_row = jnp.concatenate(
        [
            fwd_lower[-1][None],
            jnp.ones((1, lines_here), jnp.float32),
            fwd_upper[-1][None],
            fwd_right[-1],
        ],
        axis=0,
    )
    reduced = jnp.stack([first_row, last_row])
    chunk = lines_here // n_pencil
    sent_rows = reduced.reshape(2, 6, n_pencil, chunk).transpose(2, 0, 1, 3)
    all_rows = lax.all_to_all(sent_rows, "pencil", 0, 0, tiled=True)
    all_rows = all_rows.reshape(2 * n_pencil, 6, chunk)
    scaled_upper = []
    scaled_right = []
    carry_upper = jnp.zeros((chunk,), jnp.float32)
    carry_right = jnp.zeros((3, chunk), jnp.float32)
    for row_at in range(2 * n_pencil):
        row_lower = all_rows[row_at, 0]
        row_inv = 1.0 / (all_rows[row_at, 1] - row_lower * carry_upper)
        carry_upper = all_rows[row_at, 2] * row_inv
        carry_right = (all_rows[row_at, 3:] - row_lower[None, :] * carry_right) * row_inv[None, :]
        scaled_upper.append(carry_upper)
        scaled_right.append(carry_right)
    ends = [None] * (2 * n_pencil)
    ends[-1] = scaled_right[-1]
    for row_at in range(2 * n_pencil - 2, -1, -1):
        ends[row_at] = scaled_right[row_at] - scaled_upper[row_at][None, :] * ends[row_at + 1]
    solved_ends = jnp.stack(ends).reshape(n_pencil, 2, 3, chunk)
    solved_ends = lax.all_to_all(solved_ends, "pencil", 0, 0, tiled=True)
    solution_ends = solved_ends.transpose(1, 2, 0, 3).reshape(2, 3, lines_here)
    end_first = solution_ends[0]
    end_last = solution_ends[1]
    columns = [end_first]
    for index_k in range(seg_width - 2):
        columns.append(
            back_right[index_k]
            - back_lower[index_k][None, :] * end_first
            - back_upper[index_k][None, :] * end_last
        )
    columns.append(end_last)
    return jnp.stack(columns, axis=1)


def solution(mesh):
    in_specs = (
        P(("pencil", "group"), None, None),
        P(("pencil", "group"), None),
        P(("pencil", "group"), None),
        P(("pencil", "group")),
    )
    out_specs = P(None, "pencil", "group")
    return jax.shard_map(
        on_device, mesh=mesh, in_specs=in_specs, out_specs=out_specs, check_vma=False
    )
```

```python
import jax
import jax.numpy as jnp
from jax import lax
from jax.sharding import PartitionSpec as P

EDGE = 8
CELLS = 512
BX_SEG = 3
LB_DEV = 128
BPD = 384


def shifted(value, axis, steps):
    count = lax.axis_size(axis)
    first, last = (max(0, -steps), min(count, count - steps))
    return lax.ppermute(value, axis, [(source, source + steps) for source in range(first, last)])


def padded(block, sides, width):
    for axis, dim in sides:
        count = lax.axis_size(axis)
        forward = [(i, i + 1) for i in range(count - 1)]
        backward = [(target, source) for source, target in forward]
        low = lax.ppermute(
            lax.slice_in_dim(block, block.shape[dim] - width, None, axis=dim), axis, forward
        )
        high = lax.ppermute(lax.slice_in_dim(block, 0, width, axis=dim), axis, backward)
        block = jnp.concatenate([low, block, high], axis=dim)
    return block


def combine_rows(row_set, before, after_rows, left_ok, right_ok):
    alpha = jnp.where(
        left_ok, -row_set[..., 0, :] / jnp.where(left_ok, before[..., 1, :], 1.0), 0.0
    )
    gamma = jnp.where(
        right_ok, -row_set[..., 2, :] / jnp.where(right_ok, after_rows[..., 1, :], 1.0), 0.0
    )
    new_lower = alpha * before[..., 0, :]
    new_upper = gamma * after_rows[..., 2, :]
    new_main = row_set[..., 1, :] + alpha * before[..., 2, :] + gamma * after_rows[..., 0, :]
    new_right = (
        row_set[..., 3:, :]
        + alpha[..., None, :] * before[..., 3:, :]
        + gamma[..., None, :] * after_rows[..., 3:, :]
    )
    return jnp.concatenate(
        [new_lower[..., None, :], new_main[..., None, :], new_upper[..., None, :], new_right],
        axis=-2,
    )


def neighbours(left_part, right_part, offset):
    from_left = shifted(left_part, "pencil", offset)
    from_right = shifted(right_part, "pencil", -offset)
    return (from_left, from_right)


def on_device(velocity, viscosity, density, slot_block):
    n_pencil = lax.axis_size("pencil")
    n_group = lax.axis_size("group")
    devices = n_pencil * n_group
    n_slots = slot_block.shape[0]
    capacity = n_slots // devices
    blocks_x = BX_SEG * n_pencil
    edge_sq = EDGE * EDGE
    seg_width = EDGE * BX_SEG
    lines_here = LB_DEV * edge_sq
    live_slot = slot_block >= 0
    safe_ids = jnp.where(live_slot, slot_block, 0)
    block_x = safe_ids % blocks_x
    block_line = safe_ids // blocks_x
    target = block_x // BX_SEG * n_group + block_line // LB_DEV
    one_hot = jnp.logical_and(
        target[:, None] == jnp.arange(devices, dtype=jnp.int32)[None, :], live_slot[:, None]
    ).astype(jnp.int32)
    target_rank = jnp.sum((jnp.cumsum(one_hot, axis=0) - 1) * one_hot, axis=1)
    position = jnp.where(live_slot, target * capacity + target_rank, devices * capacity)
    source_of = (
        jnp.full((devices * capacity,), n_slots, jnp.int32)
        .at[position]
        .set(jnp.arange(n_slots, dtype=jnp.int32), mode="drop")
    )
    lane_rows = CELLS // 128
    send_flow = jnp.take(velocity.reshape(n_slots, 3 * lane_rows, 128), source_of, axis=0, mode="clip")
    pair = jnp.stack([viscosity, density], axis=1).reshape(n_slots, 2 * lane_rows, 128)
    send_pair = jnp.take(pair, source_of, axis=0, mode="clip")
    labels = jnp.take(slot_block, source_of, axis=0, mode="fill", fill_value=-1)
    label_row = jnp.pad(
        labels.reshape(devices, 1, capacity).astype(jnp.float32), ((0, 0), (0, 0), (0, 128 - capacity))
    )
    send_pair = jnp.concatenate(
        [send_pair.reshape(devices, capacity * 2 * lane_rows, 128), label_row], axis=1
    )
    got_pair = lax.all_to_all(send_pair, ("pencil", "group"), 0, 0, tiled=True)
    got_pair, send_flow = lax.optimization_barrier((got_pair, send_flow))
    got_flow = lax.all_to_all(
        send_flow.reshape(devices, capacity * 3 * lane_rows, 128),
        ("pencil", "group"),
        split_axis=0,
        concat_axis=0,
        tiled=True,
    )
    n_arrived = devices * capacity
    arrived_ids = got_pair[:, capacity * 2 * lane_rows, :capacity].astype(jnp.int32).reshape(n_arrived)
    got_pair = got_pair[:, : capacity * 2 * lane_rows].reshape(n_arrived, 2, CELLS)
    got_flow = got_flow.reshape(n_arrived, 3, CELLS)
    got_visc = got_pair[:, 0]
    got_mass = got_pair[:, 1]
    pencil_at = lax.axis_index("pencil")
    group_at = lax.axis_index("group")
    arrive_live = arrived_ids >= 0
    arrive_safe = jnp.where(arrive_live, arrived_ids, 0)
    local_block = (arrive_safe // blocks_x - group_at * LB_DEV) * BX_SEG + (
        arrive_safe % blocks_x - pencil_at * BX_SEG
    )
    local_block = jnp.where(arrive_live, local_block, BPD).astype(jnp.int32)
    which_arrived = (
        jnp.full((BPD,), n_arrived, jnp.int32)
        .at[local_block]
        .set(jnp.arange(n_arrived, dtype=jnp.int32), mode="drop")
    )
    block_active = (which_arrived < n_arrived).astype(jnp.float32)
    tile_flow = jnp.take(got_flow, which_arrived, axis=0, mode="clip")
    tile_visc = jnp.take(got_visc, which_arrived, axis=0, mode="clip")
    tile_mass = jnp.take(got_mass, which_arrived, axis=0, mode="fill", fill_value=0.0)
    flow_grid = (
        tile_flow.reshape(LB_DEV, BX_SEG, 3, EDGE, edge_sq)
        .transpose(2, 1, 3, 0, 4)
        .reshape(3, seg_width, lines_here)
    )
    visc_grid = (
        tile_visc.reshape(LB_DEV, BX_SEG, EDGE, edge_sq)
        .transpose(1, 2, 0, 3)
        .reshape(seg_width, lines_here)
    )
    mass_grid = (
        tile_mass.reshape(LB_DEV, BX_SEG, EDGE, edge_sq)
        .transpose(1, 2, 0, 3)
        .reshape(seg_width, lines_here)
    )
    active = jnp.broadcast_to(
        block_active.reshape(LB_DEV, BX_SEG).T[:, None, :, None], (BX_SEG, EDGE, LB_DEV, edge_sq)
    ).reshape(seg_width, lines_here)
    rimmed = padded(jnp.stack([visc_grid, active], axis=0), (("pencil", 1),), 1)
    face_visc = 0.5 * (rimmed[0, :-1] + rimmed[0, 1:]) * rimmed[1, :-1] * rimmed[1, 1:]
    face_left = face_visc[:-1]
    face_right = face_visc[1:]
    lower_band = -face_left
    upper_band = -face_right
    main_band = mass_grid + face_left + face_right + (1.0 - active)
    right_side = mass_grid[None] * flow_grid
    prev_lower = -jnp.ones((lines_here,), jnp.float32)
    prev_upper = jnp.zeros((lines_here,), jnp.float32)
    prev_right = jnp.zeros((3, lines_here), jnp.float32)
    fwd_lower, fwd_upper, fwd_right = ([], [], [])
    for cell_x in range(1, seg_width):
        low_coef = lower_band[cell_x]
        pivot_inv = 1.0 / (main_band[cell_x] - low_coef * prev_upper)
        prev_lower = -low_coef * prev_lower * pivot_inv
        prev_upper = upper_band[cell_x] * pivot_inv
        prev_right = (right_side[:, cell_x] - low_coef[None, :] * prev_right) * pivot_inv[None, :]
        fwd_lower.append(prev_lower)
        fwd_upper.append(prev_upper)
        fwd_right.append(prev_right)
    next_lower = jnp.zeros((lines_here,), jnp.float32)
    next_upper = -jnp.ones((lines_here,), jnp.float32)
    next_right = jnp.zeros((3, lines_here), jnp.float32)
    back_lower = [None] * (seg_width - 2)
    back_upper = [None] * (seg_width - 2)
    back_right = [None] * (seg_width - 2)
    for index_k in range(seg_width - 3, -1, -1):
        row_upper = fwd_upper[index_k]
        next_right = fwd_right[index_k] - row_upper[None, :] * next_right
        next_lower = fwd_lower[index_k] - row_upper * next_lower
        next_upper = -row_upper * next_upper
        back_lower[index_k] = next_lower
        back_upper[index_k] = next_upper
        back_right[index_k] = next_right
    first_row = jnp.concatenate(
        [
            lower_band[0][None],
            (main_band[0] - upper_band[0] * back_lower[0])[None],
            (-upper_band[0] * back_upper[0])[None],
            right_side[:, 0] - upper_band[0][None, :] * back_right[0],
        ],
        axis=0,
    )
    last_row = jnp.concatenate(
        [
            fwd_lower[-1][None],
            jnp.ones((1, lines_here), jnp.float32),
            fwd_upper[-1][None],
            fwd_right[-1],
        ],
        axis=0,
    )
    reduced = jnp.stack([first_row, last_row])
    chunk = lines_here // n_pencil
    sent_rows = reduced.reshape(2, 6, n_pencil, chunk).transpose(2, 0, 1, 3)
    all_rows = lax.all_to_all(sent_rows, "pencil", 0, 0, tiled=True)
    all_rows = all_rows.reshape(2 * n_pencil, 6, chunk)
    scaled_upper = []
    scaled_right = []
    carry_upper = jnp.zeros((chunk,), jnp.float32)
    carry_right = jnp.zeros((3, chunk), jnp.float32)
    for row_at in range(2 * n_pencil):
        row_lower = all_rows[row_at, 0]
        row_inv = 1.0 / (all_rows[row_at, 1] - row_lower * carry_upper)
        carry_upper = all_rows[row_at, 2] * row_inv
        carry_right = (all_rows[row_at, 3:] - row_lower[None, :] * carry_right) * row_inv[None, :]
        scaled_upper.append(carry_upper)
        scaled_right.append(carry_right)
    ends = [None] * (2 * n_pencil)
    ends[-1] = scaled_right[-1]
    for row_at in range(2 * n_pencil - 2, -1, -1):
        ends[row_at] = scaled_right[row_at] - scaled_upper[row_at][None, :] * ends[row_at + 1]
    solved_ends = jnp.stack(ends).reshape(n_pencil, 2, 3, chunk)
    solved_ends = lax.all_to_all(solved_ends, "pencil", 0, 0, tiled=True)
    solution_ends = solved_ends.transpose(1, 2, 0, 3).reshape(2, 3, lines_here)
    end_first = solution_ends[0]
    end_last = solution_ends[1]
    inner_lower = jnp.stack(back_lower, axis=0)
    inner_upper = jnp.stack(back_upper, axis=0)
    planes = []
    for comp in range(3):
        inner = (
            jnp.stack([row[comp] for row in back_right], axis=0)
            - inner_lower * end_first[comp][None, :]
            - inner_upper * end_last[comp][None, :]
        )
        planes.append(
            jnp.concatenate([end_first[comp][None, :], inner, end_last[comp][None, :]], axis=0)
        )
    return jnp.stack(planes, axis=0)


def solution(mesh):
    in_specs = (
        P(("pencil", "group"), None, None),
        P(("pencil", "group"), None),
        P(("pencil", "group"), None),
        P(("pencil", "group")),
    )
    out_specs = P(None, "pencil", "group")
    return jax.shard_map(
        on_device, mesh=mesh, in_specs=in_specs, out_specs=out_specs, check_vma=False
    )
```

```python
import jax
import jax.numpy as jnp
from jax import lax
from jax.sharding import PartitionSpec as P

EDGE = 8
CELLS = 512
BX_SEG = 3
LB_DEV = 128
BPD = 384


def shifted(value, axis, steps):
    count = lax.axis_size(axis)
    first, last = (max(0, -steps), min(count, count - steps))
    return lax.ppermute(value, axis, [(source, source + steps) for source in range(first, last)])


def padded(block, sides, width):
    for axis, dim in sides:
        count = lax.axis_size(axis)
        forward = [(i, i + 1) for i in range(count - 1)]
        backward = [(target, source) for source, target in forward]
        low = lax.ppermute(
            lax.slice_in_dim(block, block.shape[dim] - width, None, axis=dim), axis, forward
        )
        high = lax.ppermute(lax.slice_in_dim(block, 0, width, axis=dim), axis, backward)
        block = jnp.concatenate([low, block, high], axis=dim)
    return block


def combine_rows(row_set, before, after_rows, left_ok, right_ok):
    alpha = jnp.where(
        left_ok, -row_set[..., 0, :] / jnp.where(left_ok, before[..., 1, :], 1.0), 0.0
    )
    gamma = jnp.where(
        right_ok, -row_set[..., 2, :] / jnp.where(right_ok, after_rows[..., 1, :], 1.0), 0.0
    )
    new_lower = alpha * before[..., 0, :]
    new_upper = gamma * after_rows[..., 2, :]
    new_main = row_set[..., 1, :] + alpha * before[..., 2, :] + gamma * after_rows[..., 0, :]
    new_right = (
        row_set[..., 3:, :]
        + alpha[..., None, :] * before[..., 3:, :]
        + gamma[..., None, :] * after_rows[..., 3:, :]
    )
    return jnp.concatenate(
        [new_lower[..., None, :], new_main[..., None, :], new_upper[..., None, :], new_right],
        axis=-2,
    )


def neighbours(left_part, right_part, offset):
    from_left = shifted(left_part, "pencil", offset)
    from_right = shifted(right_part, "pencil", -offset)
    return (from_left, from_right)


def on_device(velocity, viscosity, density, slot_block):
    n_pencil = lax.axis_size("pencil")
    n_group = lax.axis_size("group")
    devices = n_pencil * n_group
    n_slots = slot_block.shape[0]
    capacity = n_slots // devices
    blocks_x = BX_SEG * n_pencil
    edge_sq = EDGE * EDGE
    seg_width = EDGE * BX_SEG
    lines_here = LB_DEV * edge_sq
    live_slot = slot_block >= 0
    safe_ids = jnp.where(live_slot, slot_block, 0)
    block_x = safe_ids % blocks_x
    block_line = safe_ids // blocks_x
    target = block_x // BX_SEG * n_group + block_line // LB_DEV
    one_hot = jnp.logical_and(
        target[:, None] == jnp.arange(devices, dtype=jnp.int32)[None, :], live_slot[:, None]
    ).astype(jnp.int32)
    target_rank = jnp.sum((jnp.cumsum(one_hot, axis=0) - 1) * one_hot, axis=1)
    position = jnp.where(live_slot, target * capacity + target_rank, devices * capacity)
    source_of = (
        jnp.full((devices * capacity,), n_slots, jnp.int32)
        .at[position]
        .set(jnp.arange(n_slots, dtype=jnp.int32), mode="drop")
    )
    lane_rows = CELLS // 128
    send_flow = jnp.take(velocity.reshape(n_slots, 3 * lane_rows, 128), source_of, axis=0, mode="clip")
    pair = jnp.stack([viscosity, density], axis=1).reshape(n_slots, 2 * lane_rows, 128)
    send_pair = jnp.take(pair, source_of, axis=0, mode="clip")
    labels = jnp.take(slot_block, source_of, axis=0, mode="fill", fill_value=-1)
    label_row = jnp.pad(
        labels.reshape(devices, 1, capacity).astype(jnp.float32), ((0, 0), (0, 0), (0, 128 - capacity))
    )
    send_pair = jnp.concatenate(
        [send_pair.reshape(devices, capacity * 2 * lane_rows, 128), label_row], axis=1
    )
    got_pair = lax.all_to_all(send_pair, ("pencil", "group"), 0, 0, tiled=True)
    got_pair, send_flow = lax.optimization_barrier((got_pair, send_flow))
    got_flow = lax.all_to_all(
        send_flow.reshape(devices, capacity * 3 * lane_rows, 128),
        ("pencil", "group"),
        split_axis=0,
        concat_axis=0,
        tiled=True,
    )
    n_arrived = devices * capacity
    arrived_ids = got_pair[:, capacity * 2 * lane_rows, :capacity].astype(jnp.int32).reshape(n_arrived)
    got_pair = got_pair[:, : capacity * 2 * lane_rows].reshape(n_arrived, 2, CELLS)
    got_flow = got_flow.reshape(n_arrived, 3, CELLS)
    got_visc = got_pair[:, 0]
    got_mass = got_pair[:, 1]
    pencil_at = lax.axis_index("pencil")
    group_at = lax.axis_index("group")
    arrive_live = arrived_ids >= 0
    arrive_safe = jnp.where(arrive_live, arrived_ids, 0)
    local_block = (arrive_safe // blocks_x - group_at * LB_DEV) * BX_SEG + (
        arrive_safe % blocks_x - pencil_at * BX_SEG
    )
    local_block = jnp.where(arrive_live, local_block, BPD).astype(jnp.int32)
    which_arrived = (
        jnp.full((BPD,), n_arrived, jnp.int32)
        .at[local_block]
        .set(jnp.arange(n_arrived, dtype=jnp.int32), mode="drop")
    )
    block_active = (which_arrived < n_arrived).astype(jnp.float32)
    tile_flow = jnp.take(got_flow, which_arrived, axis=0, mode="clip")
    tile_visc = jnp.take(got_visc, which_arrived, axis=0, mode="clip")
    tile_mass = jnp.take(got_mass, which_arrived, axis=0, mode="fill", fill_value=0.0)
    flow_grid = (
        tile_flow.reshape(LB_DEV, BX_SEG, 3, EDGE, edge_sq)
        .transpose(2, 1, 3, 0, 4)
        .reshape(3, seg_width, lines_here)
    )
    visc_grid = (
        tile_visc.reshape(LB_DEV, BX_SEG, EDGE, edge_sq)
        .transpose(1, 2, 0, 3)
        .reshape(seg_width, lines_here)
    )
    mass_grid = (
        tile_mass.reshape(LB_DEV, BX_SEG, EDGE, edge_sq)
        .transpose(1, 2, 0, 3)
        .reshape(seg_width, lines_here)
    )
    active = jnp.broadcast_to(
        block_active.reshape(LB_DEV, BX_SEG).T[:, None, :, None], (BX_SEG, EDGE, LB_DEV, edge_sq)
    ).reshape(seg_width, lines_here)
    rimmed = padded(jnp.stack([visc_grid, active], axis=0), (("pencil", 1),), 1)
    face_visc = 0.5 * (rimmed[0, :-1] + rimmed[0, 1:]) * rimmed[1, :-1] * rimmed[1, 1:]
    face_left = face_visc[:-1]
    face_right = face_visc[1:]
    lower_band = -face_left
    upper_band = -face_right
    main_band = mass_grid + face_left + face_right + (1.0 - active)
    right_side = mass_grid[None] * flow_grid
    prev_lower = -jnp.ones((lines_here,), jnp.float32)
    prev_upper = jnp.zeros((lines_here,), jnp.float32)
    prev_right = jnp.zeros((3, lines_here), jnp.float32)
    fwd_lower, fwd_upper, fwd_right = ([], [], [])
    for cell_x in range(1, seg_width):
        low_coef = lower_band[cell_x]
        pivot_inv = 1.0 / (main_band[cell_x] - low_coef * prev_upper)
        prev_lower = -low_coef * prev_lower * pivot_inv
        prev_upper = upper_band[cell_x] * pivot_inv
        prev_right = (right_side[:, cell_x] - low_coef[None, :] * prev_right) * pivot_inv[None, :]
        fwd_lower.append(prev_lower)
        fwd_upper.append(prev_upper)
        fwd_right.append(prev_right)
    next_lower = jnp.zeros((lines_here,), jnp.float32)
    next_upper = -jnp.ones((lines_here,), jnp.float32)
    next_right = jnp.zeros((3, lines_here), jnp.float32)
    back_lower = [None] * (seg_width - 2)
    back_upper = [None] * (seg_width - 2)
    back_right = [None] * (seg_width - 2)
    for index_k in range(seg_width - 3, -1, -1):
        row_upper = fwd_upper[index_k]
        next_right = fwd_right[index_k] - row_upper[None, :] * next_right
        next_lower = fwd_lower[index_k] - row_upper * next_lower
        next_upper = -row_upper * next_upper
        back_lower[index_k] = next_lower
        back_upper[index_k] = next_upper
        back_right[index_k] = next_right
    first_row = jnp.concatenate(
        [
            lower_band[0][None],
            (main_band[0] - upper_band[0] * back_lower[0])[None],
            (-upper_band[0] * back_upper[0])[None],
            right_side[:, 0] - upper_band[0][None, :] * back_right[0],
        ],
        axis=0,
    )
    last_row = jnp.concatenate(
        [
            fwd_lower[-1][None],
            jnp.ones((1, lines_here), jnp.float32),
            fwd_upper[-1][None],
            fwd_right[-1],
        ],
        axis=0,
    )
    reduced = jnp.stack([first_row, last_row])
    chunk = lines_here // n_pencil
    sent_rows = reduced.reshape(2, 6, n_pencil, chunk).transpose(2, 0, 1, 3)
    all_rows = lax.all_to_all(sent_rows, "pencil", 0, 0, tiled=True)
    all_rows = all_rows.reshape(2 * n_pencil, 6, chunk)
    scaled_upper = []
    scaled_right = []
    carry_upper = jnp.zeros((chunk,), jnp.float32)
    carry_right = jnp.zeros((3, chunk), jnp.float32)
    for row_at in range(2 * n_pencil):
        row_lower = all_rows[row_at, 0]
        row_inv = 1.0 / (all_rows[row_at, 1] - row_lower * carry_upper)
        carry_upper = all_rows[row_at, 2] * row_inv
        carry_right = (all_rows[row_at, 3:] - row_lower[None, :] * carry_right) * row_inv[None, :]
        scaled_upper.append(carry_upper)
        scaled_right.append(carry_right)
    ends = [None] * (2 * n_pencil)
    ends[-1] = scaled_right[-1]
    for row_at in range(2 * n_pencil - 2, -1, -1):
        ends[row_at] = scaled_right[row_at] - scaled_upper[row_at][None, :] * ends[row_at + 1]
    solved_ends = jnp.stack(ends).reshape(n_pencil, 2, 3, chunk)
    solved_ends = lax.all_to_all(solved_ends, "pencil", 0, 0, tiled=True)
    solution_ends = solved_ends.transpose(1, 2, 0, 3).reshape(2, 3, lines_here)
    end_first = solution_ends[0]
    end_last = solution_ends[1]
    out_rows = []
    for comp in range(3):
        out_rows.append(end_first[comp])
        for index_k in range(seg_width - 2):
            out_rows.append(
                back_right[index_k][comp]
                - back_lower[index_k] * end_first[comp]
                - back_upper[index_k] * end_last[comp]
            )
        out_rows.append(end_last[comp])
    return jnp.stack(out_rows, axis=0).reshape(3, seg_width, lines_here)


def solution(mesh):
    in_specs = (
        P(("pencil", "group"), None, None),
        P(("pencil", "group"), None),
        P(("pencil", "group"), None),
        P(("pencil", "group")),
    )
    out_specs = P(None, "pencil", "group")
    return jax.shard_map(
        on_device, mesh=mesh, in_specs=in_specs, out_specs=out_specs, check_vma=False
    )
```

```python
import jax
import jax.numpy as jnp
from jax import lax
from jax.sharding import PartitionSpec as P

EDGE = 8
CELLS = 512
BX_SEG = 3
LB_DEV = 128
BPD = 384


def shifted(value, axis, steps):
    count = lax.axis_size(axis)
    first, last = (max(0, -steps), min(count, count - steps))
    return lax.ppermute(value, axis, [(source, source + steps) for source in range(first, last)])


def padded(block, sides, width):
    for axis, dim in sides:
        count = lax.axis_size(axis)
        forward = [(i, i + 1) for i in range(count - 1)]
        backward = [(target, source) for source, target in forward]
        low = lax.ppermute(
            lax.slice_in_dim(block, block.shape[dim] - width, None, axis=dim), axis, forward
        )
        high = lax.ppermute(lax.slice_in_dim(block, 0, width, axis=dim), axis, backward)
        block = jnp.concatenate([low, block, high], axis=dim)
    return block


def combine_rows(row_set, before, after_rows, left_ok, right_ok):
    alpha = jnp.where(
        left_ok, -row_set[..., 0, :] / jnp.where(left_ok, before[..., 1, :], 1.0), 0.0
    )
    gamma = jnp.where(
        right_ok, -row_set[..., 2, :] / jnp.where(right_ok, after_rows[..., 1, :], 1.0), 0.0
    )
    new_lower = alpha * before[..., 0, :]
    new_upper = gamma * after_rows[..., 2, :]
    new_main = row_set[..., 1, :] + alpha * before[..., 2, :] + gamma * after_rows[..., 0, :]
    new_right = (
        row_set[..., 3:, :]
        + alpha[..., None, :] * before[..., 3:, :]
        + gamma[..., None, :] * after_rows[..., 3:, :]
    )
    return jnp.concatenate(
        [new_lower[..., None, :], new_main[..., None, :], new_upper[..., None, :], new_right],
        axis=-2,
    )


def neighbours(left_part, right_part, offset):
    from_left = shifted(left_part, "pencil", offset)
    from_right = shifted(right_part, "pencil", -offset)
    return (from_left, from_right)


def on_device(velocity, viscosity, density, slot_block):
    n_pencil = lax.axis_size("pencil")
    n_group = lax.axis_size("group")
    devices = n_pencil * n_group
    n_slots = slot_block.shape[0]
    capacity = n_slots // devices
    blocks_x = BX_SEG * n_pencil
    edge_sq = EDGE * EDGE
    seg_width = EDGE * BX_SEG
    lines_here = LB_DEV * edge_sq
    live_slot = slot_block >= 0
    safe_ids = jnp.where(live_slot, slot_block, 0)
    block_x = safe_ids % blocks_x
    block_line = safe_ids // blocks_x
    target = block_x // BX_SEG * n_group + block_line // LB_DEV
    one_hot = jnp.logical_and(
        target[:, None] == jnp.arange(devices, dtype=jnp.int32)[None, :], live_slot[:, None]
    ).astype(jnp.int32)
    target_rank = jnp.sum((jnp.cumsum(one_hot, axis=0) - 1) * one_hot, axis=1)
    position = jnp.where(live_slot, target * capacity + target_rank, devices * capacity)
    source_of = (
        jnp.full((devices * capacity,), n_slots, jnp.int32)
        .at[position]
        .set(jnp.arange(n_slots, dtype=jnp.int32), mode="drop")
    )
    lane_rows = CELLS // 128
    big = jnp.concatenate(
        [velocity.reshape(n_slots, 3 * lane_rows, 128), density.reshape(n_slots, lane_rows, 128)],
        axis=1,
    )
    send_big = jnp.take(big, source_of, axis=0, mode="clip")
    send_visc = jnp.take(viscosity.reshape(n_slots, lane_rows, 128), source_of, axis=0, mode="clip")
    labels = jnp.take(slot_block, source_of, axis=0, mode="fill", fill_value=-1)
    label_row = jnp.pad(
        labels.reshape(devices, 1, capacity).astype(jnp.float32), ((0, 0), (0, 0), (0, 128 - capacity))
    )
    visc_rows = capacity * lane_rows
    send_small = jnp.concatenate(
        [send_visc.reshape(devices, visc_rows, 128), label_row], axis=1
    )
    got_small = lax.all_to_all(send_small, ("pencil", "group"), 0, 0, tiled=True)
    got_small, send_big = lax.optimization_barrier((got_small, send_big))
    got_big = lax.all_to_all(
        send_big.reshape(devices, capacity * 4 * lane_rows, 128),
        ("pencil", "group"),
        split_axis=0,
        concat_axis=0,
        tiled=True,
    )
    n_arrived = devices * capacity
    arrived_ids = got_small[:, visc_rows, :capacity].astype(jnp.int32).reshape(n_arrived)
    got_big = got_big.reshape(n_arrived, 4 * lane_rows, 128)
    got_flow = got_big[:, : 3 * lane_rows].reshape(n_arrived, 3, CELLS)
    got_mass = got_big[:, 3 * lane_rows :].reshape(n_arrived, CELLS)
    got_visc = got_small[:, :visc_rows].reshape(n_arrived, CELLS)
    pencil_at = lax.axis_index("pencil")
    group_at = lax.axis_index("group")
    arrive_live = arrived_ids >= 0
    arrive_safe = jnp.where(arrive_live, arrived_ids, 0)
    local_block = (arrive_safe // blocks_x - group_at * LB_DEV) * BX_SEG + (
        arrive_safe % blocks_x - pencil_at * BX_SEG
    )
    local_block = jnp.where(arrive_live, local_block, BPD).astype(jnp.int32)
    which_arrived = (
        jnp.full((BPD,), n_arrived, jnp.int32)
        .at[local_block]
        .set(jnp.arange(n_arrived, dtype=jnp.int32), mode="drop")
    )
    block_active = (which_arrived < n_arrived).astype(jnp.float32)
    tile_flow = jnp.take(got_flow, which_arrived, axis=0, mode="clip")
    tile_visc = jnp.take(got_visc, which_arrived, axis=0, mode="clip")
    tile_mass = jnp.take(got_mass, which_arrived, axis=0, mode="fill", fill_value=0.0)
    flow_grid = (
        tile_flow.reshape(LB_DEV, BX_SEG, 3, EDGE, edge_sq)
        .transpose(2, 1, 3, 0, 4)
        .reshape(3, seg_width, lines_here)
    )
    visc_grid = (
        tile_visc.reshape(LB_DEV, BX_SEG, EDGE, edge_sq)
        .transpose(1, 2, 0, 3)
        .reshape(seg_width, lines_here)
    )
    mass_grid = (
        tile_mass.reshape(LB_DEV, BX_SEG, EDGE, edge_sq)
        .transpose(1, 2, 0, 3)
        .reshape(seg_width, lines_here)
    )
    active = jnp.broadcast_to(
        block_active.reshape(LB_DEV, BX_SEG).T[:, None, :, None], (BX_SEG, EDGE, LB_DEV, edge_sq)
    ).reshape(seg_width, lines_here)
    rimmed = padded(jnp.stack([visc_grid, active], axis=0), (("pencil", 1),), 1)
    face_visc = 0.5 * (rimmed[0, :-1] + rimmed[0, 1:]) * rimmed[1, :-1] * rimmed[1, 1:]
    face_left = face_visc[:-1]
    face_right = face_visc[1:]
    lower_band = -face_left
    upper_band = -face_right
    main_band = mass_grid + face_left + face_right + (1.0 - active)
    right_side = mass_grid[None] * flow_grid
    prev_lower = -jnp.ones((lines_here,), jnp.float32)
    prev_upper = jnp.zeros((lines_here,), jnp.float32)
    prev_right = jnp.zeros((3, lines_here), jnp.float32)
    fwd_lower, fwd_upper, fwd_right = ([], [], [])
    for cell_x in range(1, seg_width):
        low_coef = lower_band[cell_x]
        pivot_inv = 1.0 / (main_band[cell_x] - low_coef * prev_upper)
        prev_lower = -low_coef * prev_lower * pivot_inv
        prev_upper = upper_band[cell_x] * pivot_inv
        prev_right = (right_side[:, cell_x] - low_coef[None, :] * prev_right) * pivot_inv[None, :]
        fwd_lower.append(prev_lower)
        fwd_upper.append(prev_upper)
        fwd_right.append(prev_right)
    next_lower = jnp.zeros((lines_here,), jnp.float32)
    next_upper = -jnp.ones((lines_here,), jnp.float32)
    next_right = jnp.zeros((3, lines_here), jnp.float32)
    back_lower = [None] * (seg_width - 2)
    back_upper = [None] * (seg_width - 2)
    back_right = [None] * (seg_width - 2)
    for index_k in range(seg_width - 3, -1, -1):
        row_upper = fwd_upper[index_k]
        next_right = fwd_right[index_k] - row_upper[None, :] * next_right
        next_lower = fwd_lower[index_k] - row_upper * next_lower
        next_upper = -row_upper * next_upper
        back_lower[index_k] = next_lower
        back_upper[index_k] = next_upper
        back_right[index_k] = next_right
    first_row = jnp.concatenate(
        [
            lower_band[0][None],
            (main_band[0] - upper_band[0] * back_lower[0])[None],
            (-upper_band[0] * back_upper[0])[None],
            right_side[:, 0] - upper_band[0][None, :] * back_right[0],
        ],
        axis=0,
    )
    last_row = jnp.concatenate(
        [
            fwd_lower[-1][None],
            jnp.ones((1, lines_here), jnp.float32),
            fwd_upper[-1][None],
            fwd_right[-1],
        ],
        axis=0,
    )
    reduced = jnp.stack([first_row, last_row])
    chunk = lines_here // n_pencil
    sent_rows = reduced.reshape(2, 6, n_pencil, chunk).transpose(2, 0, 1, 3)
    all_rows = lax.all_to_all(sent_rows, "pencil", 0, 0, tiled=True)
    all_rows = all_rows.reshape(2 * n_pencil, 6, chunk)
    scaled_upper = []
    scaled_right = []
    carry_upper = jnp.zeros((chunk,), jnp.float32)
    carry_right = jnp.zeros((3, chunk), jnp.float32)
    for row_at in range(2 * n_pencil):
        row_lower = all_rows[row_at, 0]
        row_inv = 1.0 / (all_rows[row_at, 1] - row_lower * carry_upper)
        carry_upper = all_rows[row_at, 2] * row_inv
        carry_right = (all_rows[row_at, 3:] - row_lower[None, :] * carry_right) * row_inv[None, :]
        scaled_upper.append(carry_upper)
        scaled_right.append(carry_right)
    ends = [None] * (2 * n_pencil)
    ends[-1] = scaled_right[-1]
    for row_at in range(2 * n_pencil - 2, -1, -1):
        ends[row_at] = scaled_right[row_at] - scaled_upper[row_at][None, :] * ends[row_at + 1]
    solved_ends = jnp.stack(ends).reshape(n_pencil, 2, 3, chunk)
    solved_ends = lax.all_to_all(solved_ends, "pencil", 0, 0, tiled=True)
    solution_ends = solved_ends.transpose(1, 2, 0, 3).reshape(2, 3, lines_here)
    end_first = solution_ends[0]
    end_last = solution_ends[1]
    columns = [end_first]
    for index_k in range(seg_width - 2):
        columns.append(
            back_right[index_k]
            - back_lower[index_k][None, :] * end_first
            - back_upper[index_k][None, :] * end_last
        )
    columns.append(end_last)
    return jnp.stack(columns, axis=1)


def solution(mesh):
    in_specs = (
        P(("pencil", "group"), None, None),
        P(("pencil", "group"), None),
        P(("pencil", "group"), None),
        P(("pencil", "group")),
    )
    out_specs = P(None, "pencil", "group")
    return jax.shard_map(
        on_device, mesh=mesh, in_specs=in_specs, out_specs=out_specs, check_vma=False
    )
```

```python
import jax
import jax.numpy as jnp
from jax import lax
from jax.sharding import PartitionSpec as P

EDGE = 8
CELLS = 512
BX_SEG = 3
LB_DEV = 128
BPD = 384


def shifted(value, axis, steps):
    count = lax.axis_size(axis)
    first, last = (max(0, -steps), min(count, count - steps))
    return lax.ppermute(value, axis, [(source, source + steps) for source in range(first, last)])


def padded(block, sides, width):
    for axis, dim in sides:
        count = lax.axis_size(axis)
        forward = [(i, i + 1) for i in range(count - 1)]
        backward = [(target, source) for source, target in forward]
        low = lax.ppermute(
            lax.slice_in_dim(block, block.shape[dim] - width, None, axis=dim), axis, forward
        )
        high = lax.ppermute(lax.slice_in_dim(block, 0, width, axis=dim), axis, backward)
        block = jnp.concatenate([low, block, high], axis=dim)
    return block


def combine_rows(row_set, before, after_rows, left_ok, right_ok):
    alpha = jnp.where(
        left_ok, -row_set[..., 0, :] / jnp.where(left_ok, before[..., 1, :], 1.0), 0.0
    )
    gamma = jnp.where(
        right_ok, -row_set[..., 2, :] / jnp.where(right_ok, after_rows[..., 1, :], 1.0), 0.0
    )
    new_lower = alpha * before[..., 0, :]
    new_upper = gamma * after_rows[..., 2, :]
    new_main = row_set[..., 1, :] + alpha * before[..., 2, :] + gamma * after_rows[..., 0, :]
    new_right = (
        row_set[..., 3:, :]
        + alpha[..., None, :] * before[..., 3:, :]
        + gamma[..., None, :] * after_rows[..., 3:, :]
    )
    return jnp.concatenate(
        [new_lower[..., None, :], new_main[..., None, :], new_upper[..., None, :], new_right],
        axis=-2,
    )


def neighbours(left_part, right_part, offset):
    from_left = shifted(left_part, "pencil", offset)
    from_right = shifted(right_part, "pencil", -offset)
    return (from_left, from_right)


def on_device(velocity, viscosity, density, slot_block):
    n_pencil = lax.axis_size("pencil")
    n_group = lax.axis_size("group")
    devices = n_pencil * n_group
    n_slots = slot_block.shape[0]
    capacity = n_slots // devices
    blocks_x = BX_SEG * n_pencil
    edge_sq = EDGE * EDGE
    seg_width = EDGE * BX_SEG
    lines_here = LB_DEV * edge_sq
    live_slot = slot_block >= 0
    safe_ids = jnp.where(live_slot, slot_block, 0)
    block_x = safe_ids % blocks_x
    block_line = safe_ids // blocks_x
    target = block_x // BX_SEG * n_group + block_line // LB_DEV
    one_hot = jnp.logical_and(
        target[:, None] == jnp.arange(devices, dtype=jnp.int32)[None, :], live_slot[:, None]
    ).astype(jnp.int32)
    target_rank = jnp.sum((jnp.cumsum(one_hot, axis=0) - 1) * one_hot, axis=1)
    position = jnp.where(live_slot, target * capacity + target_rank, devices * capacity)
    source_of = (
        jnp.full((devices * capacity,), n_slots, jnp.int32)
        .at[position]
        .set(jnp.arange(n_slots, dtype=jnp.int32), mode="drop")
    )
    lane_rows = CELLS // 128
    big = jnp.concatenate(
        [velocity.reshape(n_slots, 3 * lane_rows, 128), density.reshape(n_slots, lane_rows, 128)],
        axis=1,
    )
    send_big = jnp.take(big, source_of, axis=0, mode="clip")
    send_visc = jnp.take(viscosity.reshape(n_slots, lane_rows, 128), source_of, axis=0, mode="clip")
    labels = jnp.take(slot_block, source_of, axis=0, mode="fill", fill_value=-1)
    label_row = jnp.pad(
        labels.reshape(devices, 1, capacity).astype(jnp.float32), ((0, 0), (0, 0), (0, 128 - capacity))
    )
    visc_rows = capacity * lane_rows
    send_small = jnp.concatenate(
        [send_visc.reshape(devices, visc_rows, 128), label_row], axis=1
    )
    got_small = lax.all_to_all(send_small, ("pencil", "group"), 0, 0, tiled=True)
    got_small, send_big = lax.optimization_barrier((got_small, send_big))
    got_big = lax.all_to_all(
        send_big.reshape(devices, capacity * 4 * lane_rows, 128),
        ("pencil", "group"),
        split_axis=0,
        concat_axis=0,
        tiled=True,
    )
    n_arrived = devices * capacity
    arrived_ids = got_small[:, visc_rows, :capacity].astype(jnp.int32).reshape(n_arrived)
    got_big = got_big.reshape(n_arrived, 4 * lane_rows, 128)
    got_visc = got_small[:, :visc_rows].reshape(n_arrived, CELLS)
    pencil_at = lax.axis_index("pencil")
    group_at = lax.axis_index("group")
    arrive_live = arrived_ids >= 0
    arrive_safe = jnp.where(arrive_live, arrived_ids, 0)
    local_block = (arrive_safe // blocks_x - group_at * LB_DEV) * BX_SEG + (
        arrive_safe % blocks_x - pencil_at * BX_SEG
    )
    local_block = jnp.where(arrive_live, local_block, BPD).astype(jnp.int32)
    which_arrived = (
        jnp.full((BPD,), n_arrived, jnp.int32)
        .at[local_block]
        .set(jnp.arange(n_arrived, dtype=jnp.int32), mode="drop")
    )
    block_active = (which_arrived < n_arrived).astype(jnp.float32)
    tile_big = jnp.take(got_big, which_arrived, axis=0, mode="clip")
    tile_visc = jnp.take(got_visc, which_arrived, axis=0, mode="clip")
    big_grid = (
        tile_big.reshape(LB_DEV, BX_SEG, 4, EDGE, edge_sq)
        .transpose(2, 1, 3, 0, 4)
        .reshape(4, seg_width, lines_here)
    )
    visc_grid = (
        tile_visc.reshape(LB_DEV, BX_SEG, EDGE, edge_sq)
        .transpose(1, 2, 0, 3)
        .reshape(seg_width, lines_here)
    )
    active = jnp.broadcast_to(
        block_active.reshape(LB_DEV, BX_SEG).T[:, None, :, None], (BX_SEG, EDGE, LB_DEV, edge_sq)
    ).reshape(seg_width, lines_here)
    flow_grid = big_grid[:3]
    mass_grid = jnp.where(active > 0.0, big_grid[3], 0.0)
    rimmed = padded(jnp.stack([visc_grid, active], axis=0), (("pencil", 1),), 1)
    face_visc = 0.5 * (rimmed[0, :-1] + rimmed[0, 1:]) * rimmed[1, :-1] * rimmed[1, 1:]
    face_left = face_visc[:-1]
    face_right = face_visc[1:]
    lower_band = -face_left
    upper_band = -face_right
    main_band = mass_grid + face_left + face_right + (1.0 - active)
    right_side = mass_grid[None] * flow_grid
    prev_lower = -jnp.ones((lines_here,), jnp.float32)
    prev_upper = jnp.zeros((lines_here,), jnp.float32)
    prev_right = jnp.zeros((3, lines_here), jnp.float32)
    fwd_lower, fwd_upper, fwd_right = ([], [], [])
    for cell_x in range(1, seg_width):
        low_coef = lower_band[cell_x]
        pivot_inv = 1.0 / (main_band[cell_x] - low_coef * prev_upper)
        prev_lower = -low_coef * prev_lower * pivot_inv
        prev_upper = upper_band[cell_x] * pivot_inv
        prev_right = (right_side[:, cell_x] - low_coef[None, :] * prev_right) * pivot_inv[None, :]
        fwd_lower.append(prev_lower)
        fwd_upper.append(prev_upper)
        fwd_right.append(prev_right)
    next_lower = jnp.zeros((lines_here,), jnp.float32)
    next_upper = -jnp.ones((lines_here,), jnp.float32)
    next_right = jnp.zeros((3, lines_here), jnp.float32)
    back_lower = [None] * (seg_width - 2)
    back_upper = [None] * (seg_width - 2)
    back_right = [None] * (seg_width - 2)
    for index_k in range(seg_width - 3, -1, -1):
        row_upper = fwd_upper[index_k]
        next_right = fwd_right[index_k] - row_upper[None, :] * next_right
        next_lower = fwd_lower[index_k] - row_upper * next_lower
        next_upper = -row_upper * next_upper
        back_lower[index_k] = next_lower
        back_upper[index_k] = next_upper
        back_right[index_k] = next_right
    first_row = jnp.concatenate(
        [
            lower_band[0][None],
            (main_band[0] - upper_band[0] * back_lower[0])[None],
            (-upper_band[0] * back_upper[0])[None],
            right_side[:, 0] - upper_band[0][None, :] * back_right[0],
        ],
        axis=0,
    )
    last_row = jnp.concatenate(
        [
            fwd_lower[-1][None],
            jnp.ones((1, lines_here), jnp.float32),
            fwd_upper[-1][None],
            fwd_right[-1],
        ],
        axis=0,
    )
    reduced = jnp.stack([first_row, last_row])
    chunk = lines_here // n_pencil
    sent_rows = reduced.reshape(2, 6, n_pencil, chunk).transpose(2, 0, 1, 3)
    all_rows = lax.all_to_all(sent_rows, "pencil", 0, 0, tiled=True)
    all_rows = all_rows.reshape(2 * n_pencil, 6, chunk)
    scaled_upper = []
    scaled_right = []
    carry_upper = jnp.zeros((chunk,), jnp.float32)
    carry_right = jnp.zeros((3, chunk), jnp.float32)
    for row_at in range(2 * n_pencil):
        row_lower = all_rows[row_at, 0]
        row_inv = 1.0 / (all_rows[row_at, 1] - row_lower * carry_upper)
        carry_upper = all_rows[row_at, 2] * row_inv
        carry_right = (all_rows[row_at, 3:] - row_lower[None, :] * carry_right) * row_inv[None, :]
        scaled_upper.append(carry_upper)
        scaled_right.append(carry_right)
    ends = [None] * (2 * n_pencil)
    ends[-1] = scaled_right[-1]
    for row_at in range(2 * n_pencil - 2, -1, -1):
        ends[row_at] = scaled_right[row_at] - scaled_upper[row_at][None, :] * ends[row_at + 1]
    solved_ends = jnp.stack(ends).reshape(n_pencil, 2, 3, chunk)
    solved_ends = lax.all_to_all(solved_ends, "pencil", 0, 0, tiled=True)
    solution_ends = solved_ends.transpose(1, 2, 0, 3).reshape(2, 3, lines_here)
    end_first = solution_ends[0]
    end_last = solution_ends[1]
    columns = [end_first]
    for index_k in range(seg_width - 2):
        columns.append(
            back_right[index_k]
            - back_lower[index_k][None, :] * end_first
            - back_upper[index_k][None, :] * end_last
        )
    columns.append(end_last)
    return jnp.stack(columns, axis=1)


def solution(mesh):
    in_specs = (
        P(("pencil", "group"), None, None),
        P(("pencil", "group"), None),
        P(("pencil", "group"), None),
        P(("pencil", "group")),
    )
    out_specs = P(None, "pencil", "group")
    return jax.shard_map(
        on_device, mesh=mesh, in_specs=in_specs, out_specs=out_specs, check_vma=False
    )
```
